256 devices in a mesh: die: 2 (over z_lo), row: 16 (over z_hi, x), col: 8 (over y, core).
Axes of the slice: x: 4, y: 4, z: 8 (z_hi: 4, z_lo: 2; z = z_hi * 2 + z_lo), core: 2. Of those that a mesh axis runs over, the one named last changes fastest.
Arguments:
- old_voltage: float32 [2, 4, 2048, 8192], P(None, 'die', 'row', 'col'), may hold values from 0 to 1
- capacitance: float32 [2, 4, 2048, 8192], P(None, 'die', 'row', 'col'), may hold values from 1 to 4
- east_conductance: float32 [2, 4, 2048, 8192], P(None, 'die', 'row', 'col'), may hold values from 0.25 to 2
- south_conductance: float32 [2, 4, 2048, 8192], P(None, 'die', 'row', 'col'), may hold values from 0.25 to 2
- through_vias: int32 [4, 16, 8, 32], P('die', 'row', 'col'), may hold values from 0 to 511, all different within a row
- via_conductance: float32 [2, 4, 16, 8, 32], P(None, 'die', 'row', 'col'), may hold values from 1 to 8
- load_patterns: int32 [4, 128, 512], P('die', 'row', 'col'), may hold values from 0 to 15
- pattern_currents: float32 [16, 256], replicated, may hold values from 0 to 4
Outputs:
- voltage: float32 [2, 4, 2048, 8192], P(None, 'die', 'row', 'col')
The draws below stay inside these ranges and needn't reach their ends.
Inputs may be any that keep to these rules, and one draw needn't show every extreme that they name: `through_vias`: the 32 entries of one tile of one die are different block numbers.
All inputs are finite; a program needn't handle non-finite values.
Results may differ from the reference program's by a relative error of at most 0.00005.
Values sent between devices are 32-bit elements; how exact they have to be, the bound alone decides.
A program may use at most 64 MiB of HBM per device.

```python
import math
import jax
import jax.numpy as jnp
from jax import lax

BS = 16
KT = 32
NPAT = 16
DIES = 4
NR = 2048
NC = 8192
NB = 512
N_ROW = 16
N_COL = 8


def touch_ends(drawn, rng, low, top_value):
    shape = drawn.shape
    index_at = [jax.random.randint(jax.random.fold_in(rng, axis), (), 0, shape[axis]) for axis in range(len(shape))]
    drawn = drawn.at[tuple(index_at)].set(low)
    longest = shape.index(max(shape))
    index_at[longest] = (index_at[longest] + 1) % shape[longest]
    return drawn.at[tuple(index_at)].set(top_value)


def levels(own_key, dims, shards, least, high):
    def one(dim, blocks):
        draws = jax.random.uniform(jax.random.fold_in(jax.random.fold_in(own_key, 6), dim), (blocks,), jnp.float32, least / len(shards), high / len(shards))
        return jnp.repeat(jnp.exp(draws), dims[dim] // blocks).reshape((-1,) + (1,) * (len(dims) - dim - 1))

    factor_of = one(*shards[0])
    for cut in shards[1:]:
        factor_of = factor_of * one(*cut)
    return factor_of


def distinct(key, rows, count, top, lift):
    order = jax.random.permutation(jax.random.fold_in(key, 1), count)
    favour = order
    for power in range(3):
        favour = favour * favour // count
    favour = favour * lift // count
    tickets = jax.random.randint(jax.random.fold_in(key, 2), (rows, count), 0, 4096) + favour
    fixed_rows = jax.random.permutation(jax.random.fold_in(key, 3), rows)[jnp.arange(count) % rows]
    tickets = jnp.where(jnp.arange(rows)[:, None] == fixed_rows[None, :], 1 << 14, tickets)
    merit = tickets * count + jnp.arange(count)
    return lax.top_k(merit.astype(jnp.int32), top)[1].astype(jnp.int32)


def setup_inputs(seed: int = 0) -> dict:
    key_list = jax.random.split(jax.random.key(seed), 9)
    return {
        "old_voltage": jnp.clip(1.0 * jax.random.uniform(key_list[0], (2, DIES, NR, NC), jnp.float32) ** levels(key_list[0], (2, DIES, NR, NC), ((1, 2), (2, 16), (3, 8)), -0.2, 0.2), 0.0, 1.0),
        "capacitance": jnp.clip(jnp.exp(math.log(4.0) - 1.3862944 * jax.random.uniform(key_list[1], (2, DIES, NR, NC), jnp.float32) ** levels(key_list[1], (2, DIES, NR, NC), ((1, 2), (2, 16), (3, 8)), -0.2, 0.2)), 1.0, 4.0),
        "east_conductance": jnp.clip(jnp.exp(math.log(2.0) - 2.0794415 * jax.random.uniform(key_list[2], (2, DIES, NR, NC), jnp.float32) ** levels(key_list[2], (2, DIES, NR, NC), ((1, 2), (2, 16), (3, 8)), -0.2, 0.2)), 0.25, 2.0),
        "south_conductance": jnp.clip(jnp.exp(math.log(2.0) - 2.0794415 * jax.random.uniform(key_list[3], (2, DIES, NR, NC), jnp.float32) ** levels(key_list[3], (2, DIES, NR, NC), ((1, 2), (2, 16), (3, 8)), -0.2, 0.2)), 0.25, 2.0),
        "through_vias": distinct(key_list[4], DIES * N_ROW * N_COL, NB, KT, 0).reshape((DIES, N_ROW, N_COL, KT)),
        "via_conductance": jnp.clip(jnp.exp(math.log(8.0) - 2.0794415 * jax.random.uniform(key_list[5], (2, DIES, N_ROW, N_COL, KT), jnp.float32) ** levels(key_list[5], (2, DIES, N_ROW, N_COL, KT), ((1, 2), (2, 16), (3, 8)), -0.2, 0.2)), 1.0, 8.0),
        "load_patterns": touch_ends(jax.random.randint(key_list[6], (DIES, NR // BS, NC // BS), 0, NPAT), jax.random.fold_in(key_list[6], 1), 0, NPAT - 1).astype(jnp.int32),
        "pattern_currents": jnp.clip(jax.random.uniform(key_list[7], (NPAT, BS * BS), jnp.float32, 0.0, 4.0), 0.0, 4.0),
    }


sweep_weights = (0.85, 1.35)


def place_centers(values, block):
    leading = values.shape[:-2]
    marker = (jnp.arange(block) == block // 2).astype(jnp.float32)
    spread = values[..., :, None, :, None] * marker[:, None, None] * marker
    return spread.reshape(leading + (values.shape[-2] * block, values.shape[-1] * block))


def reference(old_voltage, capacitance, east_conductance, south_conductance, through_vias, via_conductance, load_patterns, pattern_currents):
    nets, layers, grid_rows, grid_cols = old_voltage.shape
    tile_rows = grid_rows // N_ROW
    tile_cols = grid_cols // N_COL
    block_rows = tile_rows // BS
    block_cols = tile_cols // BS
    onehot = (through_vias[..., None] == jnp.arange(block_rows * block_cols)).astype(jnp.float32)
    per_tile = jnp.einsum("ndrck,drckb->ndrcb", via_conductance, onehot, precision=lax.Precision.HIGHEST)
    per_block = per_tile.reshape(nets, layers, N_ROW, N_COL, block_rows, block_cols)
    per_block = per_block.transpose(0, 1, 2, 4, 3, 5).reshape(nets, layers, N_ROW * block_rows, N_COL * block_cols)
    via_down = place_centers(per_block, BS)
    via_up = jnp.concatenate([via_down[:, 1:], jnp.zeros((nets, 1, grid_rows, grid_cols), jnp.float32)], axis=1)
    picks = (load_patterns[..., None] == jnp.arange(pattern_currents.shape[0])).astype(jnp.float32)
    current = jnp.einsum("dijp,pq->dijq", picks, pattern_currents, precision=lax.Precision.HIGHEST)
    current = current.reshape(layers, grid_rows // BS, grid_cols // BS, BS, BS).transpose(0, 1, 3, 2, 4).reshape(layers, grid_rows, grid_cols)
    col_keep = (jnp.arange(grid_cols) < grid_cols - 1).astype(jnp.float32)
    row_keep = (jnp.arange(grid_rows) < grid_rows - 1).astype(jnp.float32)[:, None]
    east = east_conductance * col_keep
    south = south_conductance * row_keep
    west = jnp.concatenate([jnp.zeros((nets, layers, grid_rows, 1), jnp.float32), east[..., :-1]], axis=3)
    north = jnp.concatenate([jnp.zeros((nets, layers, 1, grid_cols), jnp.float32), south[..., :-1, :]], axis=2)
    net_sign = jnp.array([-1.0, 1.0], jnp.float32).reshape(2, 1, 1, 1)
    supply = jnp.array([1.0, 0.0], jnp.float32).reshape(2, 1, 1, 1)
    ground = (jnp.arange(layers) == 0).astype(jnp.float32).reshape(1, layers, 1, 1)
    rhs = capacitance * old_voltage + net_sign * current[None] + (ground * supply) * via_down
    diagonal = capacitance + east + west + south + north + via_down + via_up
    volts = old_voltage
    for weight_now in sweep_weights:
        padded = jnp.pad(volts, ((0, 0), (0, 0), (1, 1), (1, 1)))
        beside = east * padded[:, :, 1:-1, 2:] + west * padded[:, :, 1:-1, :-2] + south * padded[:, :, 2:, 1:-1] + north * padded[:, :, :-2, 1:-1]
        zeros_plane = jnp.zeros((nets, 1, grid_rows, grid_cols), jnp.float32)
        below = jnp.concatenate([zeros_plane, volts[:, :-1]], axis=1)
        above = jnp.concatenate([volts[:, 1:], zeros_plane], axis=1)
        vertical = via_down * below + via_up * above
        applied = diagonal * volts - beside - vertical
        volts = volts + weight_now * (rhs - applied) / diagonal
    return volts
```

```python
import jax
import jax.numpy as jnp
from jax import lax
from jax.experimental import pallas as pl
from jax.experimental.pallas import tpu as pltpu
from jax.sharding import PartitionSpec as P

BS = 16
LANES = 128
PAD = 8
W1, W2 = 0.85, 1.35
ALPHA = 1.0 + W2 * (1.0 - W1) / W1
MESH = pl.DeviceIdType.MESH
f32 = jnp.float32


def kernel(
    u_hbm, k_hbm, e_hbm, s_hbm, sites, vias, pat_hbm, pc_hbm, out,
    us, es, ss, ks, xs, ds, ts,
    pat, pc, tab,
    snd_e, snd_w, col_w, col_e, snd_e2, snd_w2, col_w2, col_e2,
    die_snd, die_rcv, die_snd2, die_rcv2,
    load_sem, small_sem, send_sem, recv_sem,
):
    nets, layers, tiles, _, _ = es.shape
    rows = es.shape[3]
    octets = rows // 8
    block_rows = rows // BS
    die, row, col = lax.axis_index("die"), lax.axis_index("row"), lax.axis_index("col")
    n_row, n_col = lax.axis_size("row"), lax.axis_size("col")
    has_n, has_s = row > 0, row < n_row - 1
    has_w, has_e = col > 0, col < n_col - 1
    inner, cross = die, 1 - die

    small = [
        pltpu.make_async_copy(pat_hbm, pat, small_sem.at[0]),
        pltpu.make_async_copy(pc_hbm, pc, small_sem.at[1]),
    ]
    for copy in small:
        copy.start()
    planes = ((u_hbm, us, PAD), (e_hbm, es, 0), (s_hbm, ss, PAD), (k_hbm, ks, 0))
    for a, (src, dst, pad) in enumerate(planes):
        for c in range(tiles):
            pltpu.make_async_copy(
                src.at[:, :, :, c * LANES : (c + 1) * LANES],
                dst.at[:, :, c, pad : pad + rows, :],
                load_sem.at[a],
            ).start()

    def wait_load(a):
        _, dst, pad = planes[a]
        whole = dst.at[:, :, :, pad : pad + rows, :]
        pltpu.make_async_copy(whole, whole, load_sem.at[a]).wait()

    barrier = pltpu.get_barrier_semaphore()

    def greet(there, **where):
        @pl.when(there)
        def _():
            pl.semaphore_signal(barrier, inc=1, device_id=where, device_id_type=MESH)

    greet(has_n, row=row - 1)
    greet(has_s, row=row + 1)
    greet(has_w, col=col - 1)
    greet(has_e, col=col + 1)
    pl.semaphore_signal(barrier, inc=1, device_id={"die": 1 - die}, device_id_type=MESH)

    def message(i, src, dst, **where):
        return pltpu.make_async_remote_copy(
            src_ref=src,
            dst_ref=dst,
            send_sem=send_sem.at[i],
            recv_sem=recv_sem.at[i],
            device_id=where,
            device_id_type=MESH,
        )

    def last_row(ref):
        return ref.at[:, :, :, PAD + rows - 1 : PAD + rows, :]

    def first_row(ref):
        return ref.at[:, :, :, PAD : PAD + 1, :]

    def above(ref):
        return ref.at[:, :, :, PAD - 1 : PAD, :]

    def below(ref):
        return ref.at[:, :, :, PAD + rows : PAD + rows + 1, :]

    south_u = message(0, last_row(us), above(us), row=row + 1)
    south_s = message(1, last_row(ss), above(ss), row=row + 1)
    north_u = message(2, first_row(us), below(us), row=row - 1)
    east_1 = message(3, snd_e, col_w, col=col + 1)
    west_1 = message(4, snd_w, col_e, col=col - 1)
    die_1 = message(5, die_snd, die_rcv, die=1 - die)
    south_d = message(6, last_row(ds), above(ds), row=row + 1)
    north_d = message(7, first_row(ds), below(ds), row=row - 1)
    east_2 = message(8, snd_e2, col_w2, col=col + 1)
    west_2 = message(9, snd_w2, col_e2, col=col - 1)
    die_2 = message(10, die_snd2, die_rcv2, die=1 - die)

    def on(condition, *actions):
        @pl.when(condition)
        def _():
            for action in actions:
                action()

    zero_row = jnp.zeros((tiles, LANES), f32)

    def clear(side, refs, at):
        @pl.when(jnp.logical_not(side))
        def _():
            for ref in refs:
                for n in range(nets):
                    for l in range(layers):
                        ref[n, l, :, at, :] = zero_row

    clear(has_n, (us, ss, ds), PAD - 1)
    clear(has_s, (us, ds), PAD + rows)

    @pl.when(jnp.logical_not(has_w))
    def _():
        col_w[...] = jnp.zeros(col_w.shape, f32)
        col_w2[...] = jnp.zeros(col_w2.shape, f32)

    @pl.when(jnp.logical_not(has_e))
    def _():
        col_e[...] = jnp.zeros(col_e.shape, f32)
        col_e2[...] = jnp.zeros(col_e2.shape, f32)

    lane = lax.broadcasted_iota(jnp.int32, (8, LANES), 1)
    sub = lax.broadcasted_iota(jnp.int32, (8, LANES), 0)
    low = lane % BS
    group = lane // BS

    block_id = jnp.where(low < tiles, sub * (tiles * 8) + low * 8 + group, -1)
    down = [[jnp.zeros((8, LANES), f32) for _ in range(layers)] for _ in range(nets)]
    for l in range(layers):
        for i in range(sites.shape[-1]):
            here = block_id == sites[l, 0, 0, i]
            for n in range(nets):
                down[n][l] = jnp.where(here, vias[n, l, 0, 0, i], down[n][l])

    for copy in small:
        copy.wait()
    across = sub * BS + low
    halves = pc.shape[0] // 8
    for h in range(2):
        for half in range(halves):
            table = jnp.zeros((8, LANES), f32)
            for i in range(8):
                line = jnp.broadcast_to(
                    pc[half * 8 + i : half * 8 + i + 1, h * LANES : (h + 1) * LANES], (8, LANES)
                )
                table = jnp.where(group == i, jnp.take_along_axis(line, across, axis=1), table)
            tab[h, half] = table

    def currents(step, _):
        l, c = step // tiles, step % tiles
        wide = jnp.concatenate([pat[l], pat[l]], axis=1)
        number = jnp.take_along_axis(wide, c * 8 + group, axis=1) * BS + low
        tables = [[tab[h, half] for half in range(halves)] for h in range(2)]
        for b in range(block_rows):
            pick = jnp.broadcast_to(number[b : b + 1, :], (8, LANES))
            within = pick & (LANES - 1)
            upper = pick >= LANES
            for h in range(2):
                value = jnp.where(
                    upper,
                    jnp.take_along_axis(tables[h][1], within, axis=1),
                    jnp.take_along_axis(tables[h][0], within, axis=1),
                )
                at = b * BS + h * 8
                xs[0, l, c, at : at + 8, :] = -value
                xs[1, l, c, at : at + 8, :] = value
        return 0

    lax.fori_loop(0, layers * tiles, currents, 0)

    def centres(pad):
        return pl.ds(pad + BS // 2, block_rows, stride=BS)

    def gather_centres(ref, n, l):
        found = jnp.zeros((8, LANES), f32)
        for c in range(tiles):
            line = pltpu.roll(ref[n, l, c, centres(PAD), :], (c - BS // 2) % LANES, 1)
            found = jnp.where(low == c, line, found)
        return found

    def spread(packed, c):
        return jnp.where(low == BS // 2, pltpu.roll(packed, (BS // 2 - c) % LANES, 1), 0.0)

    def add_centres(ref, n, l, packed, pad, scale=None):
        for c in range(tiles):
            term = spread(packed, c)
            if scale is not None:
                term = term * scale[n, l, c, centres(0), :]
            ref[n, l, c, centres(pad), :] = ref[n, l, c, centres(pad), :] + term

    wait_load(0)
    held = [[gather_centres(us, n, l) for l in range(layers)] for n in range(nets)]
    first_die = die == 0
    for n in range(nets):
        die_snd[n] = jnp.where(first_die, held[n][1], held[n][0])
        die_snd[nets + n] = down[n][0]

    wait_load(1)

    @pl.when(jnp.logical_not(has_e))
    def _():
        for n in range(nets):
            for l in range(layers):
                def edge(o, _, n=n, l=l):
                    at = pl.ds(pl.multiple_of(o * 8, 8), 8)
                    es[n, l, tiles - 1, at, :] = jnp.where(
                        lane == LANES - 1, 0.0, es[n, l, tiles - 1, at, :]
                    )
                    return 0
                lax.fori_loop(0, octets, edge, 0)

    def pack_columns(ref, pad, send_e, send_w, with_e):
        def body(o, _):
            at = pl.multiple_of(o * 8, 8)
            to_e = jnp.zeros((8, LANES), f32)
            to_w = jnp.zeros((8, LANES), f32)
            for n in range(nets):
                for l in range(layers):
                    p = n * layers + l
                    last = ref[n, l, tiles - 1, pl.ds(at + pad, 8), :]
                    to_e = jnp.where(lane == p, pltpu.roll(last, p + 1, 1), to_e)
                    first = ref[n, l, 0, pl.ds(at + pad, 8), :]
                    to_w = jnp.where(lane == p, pltpu.roll(first, p, 1) if p else first, to_w)
                    if with_e:
                        q = nets * layers + p
                        edge = es[n, l, tiles - 1, pl.ds(at, 8), :]
                        to_e = jnp.where(lane == q, pltpu.roll(edge, q + 1, 1), to_e)
            send_e[pl.ds(at, 8), :] = to_e
            send_w[pl.ds(at, 8), :] = to_w
            return 0

        lax.fori_loop(0, octets, body, 0)

    pack_columns(us, PAD, snd_e, snd_w, True)

    wait_load(2)

    @pl.when(jnp.logical_not(has_s))
    def _():
        for n in range(nets):
            for l in range(layers):
                ss[n, l, :, PAD + rows - 1, :] = zero_row

    neighbours = 1 + sum(jnp.where(there, 1, 0) for there in (has_n, has_s, has_w, has_e))
    pl.semaphore_wait(barrier, neighbours)
    on(has_s, south_u.start, south_s.start)
    on(has_n, north_u.start)
    on(has_e, east_1.start)
    on(has_w, west_1.start)
    die_1.start()

    wait_load(3)
    for n in range(nets):
        link = down[n][1]
        package = jnp.where(first_die, down[n][0], 0.0)
        supply = 1.0 if n == 0 else 0.0
        flow = link * (held[n][1] - held[n][0])
        add_centres(ks, n, 0, link + package, 0)
        add_centres(xs, n, 0, flow + package * (supply - held[n][0]), 0)
        add_centres(ks, n, 1, link, 0)
        add_centres(xs, n, 1, -flow, 0)

    def at_lane(v, p, target):
        return pltpu.roll(v, lax.rem(target - p + LANES, LANES), 1)

    def east_of(values, c, halo):
        after = values[c + 1] if c + 1 in values else halo
        return jnp.where(lane == LANES - 1, after, values[c])

    def west_of(values, c, halo):
        before = values[c - 1] if c - 1 in values else halo
        return jnp.where(lane == 0, before, values[c])

    def span(cs, rows_at, reads):
        return [c for c in range(cs[0] - 1, cs[-1] + 2) if 0 <= c < tiles]

    def sweep_1(n, l, at, cs, halos=None, stride=None):
        def ds_(pad):
            return pl.ds(at + pad, 8) if stride is None else pl.ds(at + pad, 8, stride=stride)

        p = n * layers + l
        near = [c for c in range(cs[0] - 1, cs[-1] + 2) if 0 <= c < tiles]
        left = [c for c in near if c <= cs[-1]]
        u = {c: us[n, l, c, ds_(PAD), :] for c in near}
        e = {c: es[n, l, c, ds_(0), :] for c in left}
        turned = {c: pltpu.roll(u[c], LANES - 1, 1) for c in near}
        u_e = e_w = f_w = None
        if halos and tiles - 1 in cs:
            u_e = at_lane(col_e[ds_(0), :], p, LANES - 1)
        if halos and 0 in cs:
            e_w = at_lane(col_w[ds_(0), :], nets * layers + p, 0)
            f_w = e_w * (u[0] - at_lane(col_w[ds_(0), :], p, 0))
        flow = {}
        for c in left:
            if c + 1 in turned:
                flow[c] = e[c] * (east_of(turned, c, None) - u[c])
            else:
                flow[c] = e[c] * (east_of(turned, c, turned[c] if u_e is None else u_e) - u[c])
        flow_t = {c: pltpu.roll(flow[c], 1, 1) for c in left}
        e_t = {c: pltpu.roll(e[c], 1, 1) for c in left}
        for c in cs:
            s = ss[n, l, c, ds_(PAD), :]
            s_n = ss[n, l, c, ds_(PAD - 1), :]
            u_s = us[n, l, c, ds_(PAD + 1), :]
            u_n = us[n, l, c, ds_(PAD - 1), :]
            east_w = west_of(e_t, c, e_t[c] if e_w is None else e_w)
            flow_w = west_of(flow_t, c, flow_t[c] if f_w is None else f_w)
            diagonal = ks[n, l, c, ds_(0), :] + e[c] + east_w + s + s_n
            residual = (
                xs[n, l, c, ds_(0), :] + (flow[c] - flow_w) + (s * (u_s - u[c]) - s_n * (u[c] - u_n))
            )
            inverse = 1.0 / diagonal
            ds[n, l, c, ds_(PAD), :] = residual * (inverse * W1)
            ts[n, l, c, ds_(0), :] = inverse * W2

    def sweep_2(n, l, at, cs, halos):
        p = n * layers + l
        near = [c for c in range(cs[0] - 1, cs[-1] + 2) if 0 <= c < tiles]
        left = [c for c in near if c <= cs[-1]]
        d = {c: ds[n, l, c, pl.ds(at + PAD, 8), :] for c in near}
        e = {c: es[n, l, c, pl.ds(at, 8), :] for c in left}
        turned = {c: pltpu.roll(d[c], LANES - 1, 1) for c in near}
        d_e = g_w = None
        if halos and tiles - 1 in cs:
            d_e = at_lane(col_e2[pl.ds(at, 8), :], p, LANES - 1)
        if halos and 0 in cs:
            e_w = at_lane(col_w[pl.ds(at, 8), :], nets * layers + p, 0)
            g_w = e_w * at_lane(col_w2[pl.ds(at, 8), :], p, 0)
        pull_t = {c: pltpu.roll(e[c] * d[c], 1, 1) for c in left}
        for c in cs:
            s = ss[n, l, c, pl.ds(at + PAD, 8), :]
            s_n = ss[n, l, c, pl.ds(at + PAD - 1, 8), :]
            d_s = ds[n, l, c, pl.ds(at + PAD + 1, 8), :]
            d_n = ds[n, l, c, pl.ds(at + PAD - 1, 8), :]
            beside = (e[c] * east_of(turned, c, d_e) + west_of(pull_t, c, g_w)) + (s * d_s + s_n * d_n)
            out[n, l, pl.ds(at, 8), c * LANES : (c + 1) * LANES] = (
                us[n, l, c, pl.ds(at + PAD, 8), :] + ALPHA * d[c]
            ) + ts[n, l, c, pl.ds(at, 8), :] * beside

    middle = tuple(range(1, tiles - 1))
    every = tuple(range(tiles))
    inside = octets - 2

    def for_inside(sweep, layer, *strips, halos):
        def body(i, _):
            n, o = i // inside, 1 + i % inside
            for cs in strips:
                sweep(n, layer, pl.multiple_of(o * 8, 8), cs, halos)
            return 0

        lax.fori_loop(0, nets * inside, body, 0)

    def for_ends(sweep):
        def body(i, _):
            n, l = i // layers, i % layers
            for o in (0, octets - 1):
                sweep(n, l, o * 8, every, True)
            return 0

        lax.fori_loop(0, nets * layers, body, 0)

    for_inside(sweep_1, inner, middle, halos=False)

    die_1.wait_recv()
    across_die = [jnp.where(first_die, die_rcv[nets + n], down[n][0]) for n in range(nets)]
    for n in range(nets):
        mine = jnp.where(first_die, held[n][1], held[n][0])
        add_centres(ks, n, cross, across_die[n], 0)
        add_centres(xs, n, cross, across_die[n] * (die_rcv[n] - mine), 0)
    for n in range(nets):
        sweep_1(n, cross, BS // 2, every, stride=BS)
    moved_cross = [gather_centres(ds, n, cross) for n in range(nets)]
    for n in range(nets):
        die_snd2[n] = moved_cross[n]

    for_inside(sweep_1, cross, middle, halos=False)
    die_2.start()

    on(has_w, east_1.wait_recv)
    on(has_e, west_1.wait_recv)
    for l in range(layers):
        for_inside(sweep_1, l, (0,), (tiles - 1,), halos=True)

    on(has_n, south_u.wait_recv, south_s.wait_recv)
    on(has_s, north_u.wait_recv)
    for_ends(sweep_1)

    pack_columns(ds, PAD, snd_e2, snd_w2, False)
    on(has_s, south_d.start)
    on(has_n, north_d.start)
    on(has_e, east_2.start)
    on(has_w, west_2.start)

    moved_inner = [gather_centres(ds, n, inner) for n in range(nets)]
    for n in range(nets):
        link = down[n][1]
        add_centres(us, n, cross, link * moved_inner[n], PAD, ts)
        add_centres(us, n, inner, link * moved_cross[n], PAD, ts)
    die_2.wait_recv()
    for n in range(nets):
        add_centres(us, n, cross, across_die[n] * die_rcv2[n], PAD, ts)

    for l in range(layers):
        for_inside(sweep_2, l, middle, halos=False)
    on(has_w, east_2.wait_recv)
    on(has_e, west_2.wait_recv)
    for l in range(layers):
        for_inside(sweep_2, l, (0,), (tiles - 1,), halos=True)
    on(has_n, south_d.wait_recv)
    on(has_s, north_d.wait_recv)
    for_ends(sweep_2)

    on(has_s, south_u.wait_send, south_s.wait_send, south_d.wait_send)
    on(has_n, north_u.wait_send, north_d.wait_send)
    on(has_e, east_1.wait_send, east_2.wait_send)
    on(has_w, west_1.wait_send, west_2.wait_send)
    die_1.wait_send()
    die_2.wait_send()


def local(u, k, e, s, sites, vias, patterns, pattern_currents):
    nets, layers, rows, cols = u.shape
    tiles = cols // LANES
    grid = (nets, layers, tiles, rows, LANES)
    padded = (nets, layers, tiles, rows + 2 * PAD, LANES)
    vmem = pltpu.VMEM
    hbm = pl.BlockSpec(memory_space=pltpu.HBM)
    smem = pl.BlockSpec(memory_space=pltpu.SMEM)
    column = vmem((rows, LANES), f32)
    packed = vmem((nets, 8, LANES), f32)
    return pl.pallas_call(
        kernel,
        out_shape=vmem(u.shape, f32),
        in_specs=[hbm, hbm, hbm, hbm, smem, smem, hbm, hbm],
        out_specs=pl.BlockSpec(memory_space=vmem),
        scratch_shapes=[
            vmem(padded, f32), vmem(grid, f32), vmem(padded, f32), vmem(grid, f32),
            vmem(grid, f32), vmem(padded, f32), vmem(grid, f32),
            vmem(patterns.shape, jnp.int32), vmem(pattern_currents.shape, f32), vmem((2, 2, 8, LANES), f32),
            column, column, column, column, column, column, column, column,
            vmem((2 * nets, 8, LANES), f32), vmem((2 * nets, 8, LANES), f32), packed, packed,
            pltpu.SemaphoreType.DMA((4,)), pltpu.SemaphoreType.DMA((2,)),
            pltpu.SemaphoreType.DMA((11,)), pltpu.SemaphoreType.DMA((11,)),
        ],
        compiler_params=pltpu.CompilerParams(
            collective_id=0, has_side_effects=True, vmem_limit_bytes=64800000
        ),
    )(u, k, e, s, sites, vias, patterns, pattern_currents)


def solution(mesh):
    spec = P(None, "die", "row", "col")
    in_specs = (
        spec,
        spec,
        spec,
        spec,
        P("die", "row", "col", None),
        P(None, "die", "row", "col", None),
        P("die", "row", "col"),
        P(),
    )
    return jax.shard_map(local, mesh=mesh, in_specs=in_specs, out_specs=spec, check_vma=False)
```

```python
import jax
import jax.numpy as jnp
from jax import lax
from jax.experimental import pallas as pl
from jax.experimental.pallas import tpu as pltpu
from jax.sharding import PartitionSpec as P

BS = 16
LANES = 128
PAD = 8
W1, W2 = 0.85, 1.35
ALPHA = 1.0 + W2 * (1.0 - W1) / W1
MESH = pl.DeviceIdType.MESH
EACH_1, EACH_1C, EACH_2, EACH_2C = 7, 7, 7, 7
TILES_STEP, PACK_STEP = 4, 4
f32 = jnp.float32


def kernel(
    u_hbm, k_hbm, e_hbm, s_hbm, sites, vias, pat_hbm, pc_hbm, out,
    us, es, ss, ks, xs, ds, ts, ws,
    pat, pc, tab,
    snd_e, snd_w, col_w, col_e, snd_e2, snd_w2, col_w2, col_e2,
    die_snd, die_rcv, die_snd2, die_rcv2,
    load_sem, small_sem, send_sem, recv_sem,
):
    nets, layers, tiles, _, _ = es.shape
    rows = es.shape[3]
    octets = rows // 8
    block_rows = rows // BS
    die, row, col = lax.axis_index("die"), lax.axis_index("row"), lax.axis_index("col")
    n_row, n_col = lax.axis_size("row"), lax.axis_size("col")
    has_n, has_s = row > 0, row < n_row - 1
    has_w, has_e = col > 0, col < n_col - 1
    inner, cross = die, 1 - die

    barrier = pltpu.get_barrier_semaphore()

    def greet(there, **where):
        @pl.when(there)
        def _():
            pl.semaphore_signal(barrier, inc=1, device_id=where, device_id_type=MESH)

    greet(has_n, row=row - 1)
    greet(has_s, row=row + 1)
    greet(has_w, col=col - 1)
    greet(has_e, col=col + 1)
    pl.semaphore_signal(barrier, inc=1, device_id={"die": 1 - die}, device_id_type=MESH)

    small = [
        pltpu.make_async_copy(pat_hbm, pat, small_sem.at[0]),
        pltpu.make_async_copy(pc_hbm, pc, small_sem.at[1]),
    ]
    for copy in small:
        copy.start()
    planes = ((u_hbm, us, PAD), (e_hbm, es, 0), (s_hbm, ss, PAD), (k_hbm, ks, 0))
    for a, (src, dst, pad) in enumerate(planes):
        for c in range(tiles):
            pltpu.make_async_copy(
                src.at[:, :, :, c * LANES : (c + 1) * LANES],
                dst.at[:, :, c, pad : pad + rows, :],
                load_sem.at[a],
            ).start()

    def wait_load(a):
        _, dst, pad = planes[a]
        whole = dst.at[:, :, :, pad : pad + rows, :]
        pltpu.make_async_copy(whole, whole, load_sem.at[a]).wait()

    def message(i, src, dst, **where):
        return pltpu.make_async_remote_copy(
            src_ref=src,
            dst_ref=dst,
            send_sem=send_sem.at[i],
            recv_sem=recv_sem.at[i],
            device_id=where,
            device_id_type=MESH,
        )

    def last_row(ref):
        return ref.at[:, :, :, PAD + rows - 1 : PAD + rows, :]

    def first_row(ref):
        return ref.at[:, :, :, PAD : PAD + 1, :]

    def above(ref):
        return ref.at[:, :, :, PAD - 1 : PAD, :]

    def below(ref):
        return ref.at[:, :, :, PAD + rows : PAD + rows + 1, :]

    south_u = message(0, last_row(us), above(us), row=row + 1)
    south_s = message(1, last_row(ss), above(ss), row=row + 1)
    north_u = message(2, first_row(us), below(us), row=row - 1)
    east_1 = message(3, snd_e, col_w, col=col + 1)
    west_1 = message(4, snd_w, col_e, col=col - 1)
    die_1 = message(5, die_snd, die_rcv, die=1 - die)
    south_d = message(6, last_row(ds), above(ds), row=row + 1)
    north_d = message(7, first_row(ds), below(ds), row=row - 1)
    east_2 = message(8, snd_e2, col_w2, col=col + 1)
    west_2 = message(9, snd_w2, col_e2, col=col - 1)
    die_2 = message(10, die_snd2, die_rcv2, die=1 - die)

    def on(condition, *actions):
        @pl.when(condition)
        def _():
            for action in actions:
                action()

    zero_row = jnp.zeros((tiles, LANES), f32)

    def clear(side, refs, at):
        @pl.when(jnp.logical_not(side))
        def _():
            for ref in refs:
                for n in range(nets):
                    for l in range(layers):
                        ref[n, l, :, at, :] = zero_row

    clear(has_n, (us, ss, ds), PAD - 1)
    clear(has_s, (us, ds), PAD + rows)

    @pl.when(jnp.logical_not(has_w))
    def _():
        col_w[...] = jnp.zeros(col_w.shape, f32)
        col_w2[...] = jnp.zeros(col_w2.shape, f32)

    @pl.when(jnp.logical_not(has_e))
    def _():
        col_e[...] = jnp.zeros(col_e.shape, f32)
        col_e2[...] = jnp.zeros(col_e2.shape, f32)

    lane = lax.broadcasted_iota(jnp.int32, (8, LANES), 1)
    sub = lax.broadcasted_iota(jnp.int32, (8, LANES), 0)
    low = lane % BS
    group = lane // BS

    block_id = jnp.where(low < tiles, sub * (tiles * 8) + low * 8 + group, -1)
    down = [[jnp.zeros((8, LANES), f32) for _ in range(layers)] for _ in range(nets)]
    for l in range(layers):
        for i in range(sites.shape[-1]):
            here = block_id == sites[l, 0, 0, i]
            for n in range(nets):
                down[n][l] = jnp.where(here, vias[n, l, 0, 0, i], down[n][l])

    for copy in small:
        copy.wait()
    across = sub * BS + low
    halves = pc.shape[0] // 8
    for h in range(2):
        for half in range(halves):
            table = jnp.zeros((8, LANES), f32)
            for i in range(8):
                line = jnp.broadcast_to(
                    pc[half * 8 + i : half * 8 + i + 1, h * LANES : (h + 1) * LANES], (8, LANES)
                )
                table = jnp.where(group == i, jnp.take_along_axis(line, across, axis=1), table)
            tab[h, half] = table

    def currents(step, _):
        l = lax.div(step, tiles // TILES_STEP)
        base = lax.rem(step, tiles // TILES_STEP) * TILES_STEP
        wide = jnp.concatenate([pat[l], pat[l]], axis=1)
        tables = [[tab[h, half] for half in range(halves)] for h in range(2)]
        for k in range(TILES_STEP):
            c = base + k
            number = jnp.take_along_axis(wide, c * 8 + group, axis=1) * BS + low
            for b in range(block_rows):
                pick = jnp.broadcast_to(number[b : b + 1, :], (8, LANES))
                within = pick & (LANES - 1)
                upper = pick >= LANES
                for h in range(2):
                    value = jnp.where(
                        upper,
                        jnp.take_along_axis(tables[h][1], within, axis=1),
                        jnp.take_along_axis(tables[h][0], within, axis=1),
                    )
                    at = b * BS + h * 8
                    xs[0, l, c, at : at + 8, :] = -value
                    xs[1, l, c, at : at + 8, :] = value
        return 0

    lax.fori_loop(0, layers * tiles // TILES_STEP, currents, 0)

    def centres(pad):
        return pl.ds(pad + BS // 2, block_rows, stride=BS)

    def gather_centres(ref, n, l):
        found = jnp.zeros((8, LANES), f32)
        for c in range(tiles):
            line = pltpu.roll(ref[n, l, c, centres(PAD), :], (c - BS // 2) % LANES, 1)
            found = jnp.where(low == c, line, found)
        return found

    def spread(packed, c):
        return jnp.where(low == BS // 2, pltpu.roll(packed, (BS // 2 - c) % LANES, 1), 0.0)

    def add_centres(updates, pad):
        fresh = []
        for ref, n, l, packed, scale in updates:
            for c in range(tiles):
                term = spread(packed, c)
                if scale is not None:
                    term = term * scale[n, l, c, centres(0), :]
                fresh.append((ref, n, l, c, ref[n, l, c, centres(pad), :] + term))
        for ref, n, l, c, value in fresh:
            ref[n, l, c, centres(pad), :] = value

    wait_load(0)
    held = [[gather_centres(us, n, l) for l in range(layers)] for n in range(nets)]
    first_die = die == 0
    for n in range(nets):
        die_snd[n] = jnp.where(first_die, held[n][1], held[n][0])
        die_snd[nets + n] = down[n][0]

    wait_load(1)

    @pl.when(jnp.logical_not(has_e))
    def _():
        for n in range(nets):
            for l in range(layers):
                def edge(o, _, n=n, l=l):
                    at = pl.ds(pl.multiple_of(o * 8, 8), 8)
                    es[n, l, tiles - 1, at, :] = jnp.where(
                        lane == LANES - 1, 0.0, es[n, l, tiles - 1, at, :]
                    )
                    return 0
                lax.fori_loop(0, octets, edge, 0)

    def pack_columns(ref, pad, send_e, send_w, with_e):
        def body(step, _):
            for k in range(PACK_STEP):
                pack(pl.multiple_of(step * (8 * PACK_STEP) + k * 8, 8))
            return 0

        def pack(at):
            to_e = jnp.zeros((8, LANES), f32)
            to_w = jnp.zeros((8, LANES), f32)
            for n in range(nets):
                for l in range(layers):
                    p = n * layers + l
                    last = ref[n, l, tiles - 1, pl.ds(at + pad, 8), :]
                    to_e = jnp.where(lane == p, pltpu.roll(last, p + 1, 1), to_e)
                    first = ref[n, l, 0, pl.ds(at + pad, 8), :]
                    to_w = jnp.where(lane == p, pltpu.roll(first, p, 1) if p else first, to_w)
                    if with_e:
                        q = nets * layers + p
                        edge = es[n, l, tiles - 1, pl.ds(at, 8), :]
                        to_e = jnp.where(lane == q, pltpu.roll(edge, q + 1, 1), to_e)
            send_e[pl.ds(at, 8), :] = to_e
            send_w[pl.ds(at, 8), :] = to_w

        lax.fori_loop(0, octets // PACK_STEP, body, 0)

    pack_columns(us, PAD, snd_e, snd_w, True)

    wait_load(2)

    @pl.when(jnp.logical_not(has_s))
    def _():
        for n in range(nets):
            for l in range(layers):
                ss[n, l, :, PAD + rows - 1, :] = zero_row

    neighbours = 1 + sum(jnp.where(there, 1, 0) for there in (has_n, has_s, has_w, has_e))
    pl.semaphore_wait(barrier, neighbours)
    on(has_s, south_u.start, south_s.start)
    on(has_n, north_u.start)
    on(has_e, east_1.start)
    on(has_w, west_1.start)
    die_1.start()

    wait_load(3)
    for n in range(nets):
        link = down[n][1]
        package = jnp.where(first_die, down[n][0], 0.0)
        supply = 1.0 if n == 0 else 0.0
        flow = link * (held[n][1] - held[n][0])
        add_centres(
            [
                (ks, n, 0, link + package, None),
                (xs, n, 0, flow + package * (supply - held[n][0]), None),
                (ks, n, 1, link, None),
                (xs, n, 1, -flow, None),
            ],
            0,
        )

    def at_lane(v, p, target):
        return pltpu.roll(v, lax.rem(target - p + LANES, LANES), 1)

    def from_east(turned, c):
        return jnp.where(lane == LANES - 1, turned.get(c + 1, turned[c]), turned[c])

    def from_west(turned, c):
        return jnp.where(lane == 0, turned.get(c - 1, turned[c]), turned[c])

    def sweep_1(n, l, at, cs, halos=None, stride=None):
        def ds_(pad):
            return pl.ds(at + pad, 8) if stride is None else pl.ds(at + pad, 8, stride=stride)

        p = n * layers + l
        near = [c for c in range(cs[0] - 1, cs[-1] + 2) if 0 <= c < tiles]
        left = [c for c in near if c <= cs[-1]]
        right = [c for c in near if c >= cs[0]]
        u = {c: us[n, l, c, ds_(PAD), :] for c in near}
        e = {c: es[n, l, c, ds_(0), :] for c in left}
        u_e = {c: pltpu.roll(u[c], LANES - 1, 1) for c in right}
        u_w = {c: pltpu.roll(u[c], 1, 1) for c in left}
        e_w = {c: pltpu.roll(e[c], 1, 1) for c in left}
        if halos and tiles - 1 in cs:
            u_e[tiles] = at_lane(col_e[ds_(0), :], p, LANES - 1)
        if halos and 0 in cs:
            u_w[-1] = at_lane(col_w[ds_(0), :], p, 0)
            e_w[-1] = at_lane(col_w[ds_(0), :], nets * layers + p, 0)
        for c in cs:
            s = ss[n, l, c, ds_(PAD), :]
            s_n = ss[n, l, c, ds_(PAD - 1), :]
            u_s = us[n, l, c, ds_(PAD + 1), :]
            u_n = us[n, l, c, ds_(PAD - 1), :]
            west = from_west(e_w, c)
            diagonal = (ks[n, l, c, ds_(0), :] + e[c]) + (west + s) + s_n
            residual = (
                xs[n, l, c, ds_(0), :]
                + (e[c] * (from_east(u_e, c) - u[c]) - west * (u[c] - from_west(u_w, c)))
                + (s * (u_s - u[c]) - s_n * (u[c] - u_n))
            )
            inverse = 1.0 / diagonal
            ds[n, l, c, ds_(PAD), :] = residual * (inverse * W1)
            ts[n, l, c, ds_(0), :] = inverse * W2
            ws[n, l, c, ds_(0), :] = west

    def sweep_2(n, l, at, cs, halos):
        p = n * layers + l
        here, mid = pl.ds(at, 8), pl.ds(at + PAD, 8)
        near = [c for c in range(cs[0] - 1, cs[-1] + 2) if 0 <= c < tiles]
        d = {c: ds[n, l, c, mid, :] for c in near}
        d_e = {c: pltpu.roll(d[c], LANES - 1, 1) for c in near if c >= cs[0]}
        d_w = {c: pltpu.roll(d[c], 1, 1) for c in near if c <= cs[-1]}
        if halos and tiles - 1 in cs:
            d_e[tiles] = at_lane(col_e2[here, :], p, LANES - 1)
        if halos and 0 in cs:
            d_w[-1] = at_lane(col_w2[here, :], p, 0)
        for c in cs:
            beside = (
                es[n, l, c, here, :] * from_east(d_e, c) + ws[n, l, c, here, :] * from_west(d_w, c)
            ) + (
                ss[n, l, c, mid, :] * ds[n, l, c, pl.ds(at + PAD + 1, 8), :]
                + ss[n, l, c, pl.ds(at + PAD - 1, 8), :] * ds[n, l, c, pl.ds(at + PAD - 1, 8), :]
            )
            out[n, l, here, c * LANES : (c + 1) * LANES] = (
                us[n, l, c, mid, :] + ALPHA * d[c]
            ) + ts[n, l, c, here, :] * beside

    middle = tuple(range(1, tiles - 1))
    every = tuple(range(tiles))
    inside = octets - 2

    def for_inside(sweep, layer, *strips, halos, each):
        groups = inside // each

        def body(i, _):
            n = lax.div(i, groups)
            base = 1 + lax.rem(i, groups) * each
            for k in range(each):
                for cs in strips:
                    sweep(n, layer, pl.multiple_of((base + k) * 8, 8), cs, halos)
            return 0

        lax.fori_loop(0, nets * groups, body, 0)

    def for_ends(sweep):
        def body(i, _):
            n, l = lax.div(i, layers), lax.rem(i, layers)
            for o in (0, octets - 1):
                sweep(n, l, o * 8, every, True)
            return 0

        lax.fori_loop(0, nets * layers, body, 0)

    for_inside(sweep_1, inner, middle, halos=False, each=EACH_1)

    die_1.wait_recv()
    across_die = [jnp.where(first_die, die_rcv[nets + n], down[n][0]) for n in range(nets)]
    for n in range(nets):
        mine = jnp.where(first_die, held[n][1], held[n][0])
        add_centres(
            [
                (ks, n, cross, across_die[n], None),
                (xs, n, cross, across_die[n] * (die_rcv[n] - mine), None),
            ],
            0,
        )
    for n in range(nets):
        sweep_1(n, cross, BS // 2, every, stride=BS)
    moved_cross = [gather_centres(ds, n, cross) for n in range(nets)]
    for n in range(nets):
        die_snd2[n] = moved_cross[n]

    for_inside(sweep_1, cross, middle, halos=False, each=EACH_1)
    die_2.start()

    on(has_w, east_1.wait_recv)
    on(has_e, west_1.wait_recv)
    for l in range(layers):
        for_inside(sweep_1, l, (0,), (tiles - 1,), halos=True, each=EACH_1C)

    on(has_n, south_u.wait_recv, south_s.wait_recv)
    on(has_s, north_u.wait_recv)
    for_ends(sweep_1)

    pack_columns(ds, PAD, snd_e2, snd_w2, False)
    on(has_s, south_d.start)
    on(has_n, north_d.start)
    on(has_e, east_2.start)
    on(has_w, west_2.start)

    die_2.wait_recv()
    moved_inner = [gather_centres(ds, n, inner) for n in range(nets)]
    for n in range(nets):
        link = down[n][1]
        moved = link * moved_inner[n] + across_die[n] * die_rcv2[n]
        add_centres(
            [(us, n, cross, moved, ts), (us, n, inner, link * moved_cross[n], ts)], PAD
        )

    for l in range(layers):
        for_inside(sweep_2, l, middle, halos=False, each=EACH_2)
    on(has_w, east_2.wait_recv)
    on(has_e, west_2.wait_recv)
    for l in range(layers):
        for_inside(sweep_2, l, (0,), (tiles - 1,), halos=True, each=EACH_2C)
    on(has_n, south_d.wait_recv)
    on(has_s, north_d.wait_recv)
    for_ends(sweep_2)

    on(has_s, south_u.wait_send, south_s.wait_send, south_d.wait_send)
    on(has_n, north_u.wait_send, north_d.wait_send)
    on(has_e, east_1.wait_send, east_2.wait_send)
    on(has_w, west_1.wait_send, west_2.wait_send)
    die_1.wait_send()
    die_2.wait_send()


def local(u, k, e, s, sites, vias, patterns, pattern_currents):
    nets, layers, rows, cols = u.shape
    tiles = cols // LANES
    grid = (nets, layers, tiles, rows, LANES)
    padded = (nets, layers, tiles, rows + 2 * PAD, LANES)
    vmem = pltpu.VMEM
    hbm = pl.BlockSpec(memory_space=pltpu.HBM)
    smem = pl.BlockSpec(memory_space=pltpu.SMEM)
    column = vmem((rows, LANES), f32)
    packed = vmem((nets, 8, LANES), f32)
    return pl.pallas_call(
        kernel,
        out_shape=vmem(u.shape, f32),
        in_specs=[hbm, hbm, hbm, hbm, smem, smem, hbm, hbm],
        out_specs=pl.BlockSpec(memory_space=vmem),
        scratch_shapes=[
            vmem(padded, f32), vmem(grid, f32), vmem(padded, f32), vmem(grid, f32),
            vmem(grid, f32), vmem(padded, f32), vmem(grid, f32), vmem(grid, f32),
            vmem(patterns.shape, jnp.int32), vmem(pattern_currents.shape, f32), vmem((2, 2, 8, LANES), f32),
            column, column, column, column, column, column, column, column,
            vmem((2 * nets, 8, LANES), f32), vmem((2 * nets, 8, LANES), f32), packed, packed,
            pltpu.SemaphoreType.DMA((4,)), pltpu.SemaphoreType.DMA((2,)),
            pltpu.SemaphoreType.DMA((11,)), pltpu.SemaphoreType.DMA((11,)),
        ],
        compiler_params=pltpu.CompilerParams(
            collective_id=0, has_side_effects=True, vmem_limit_bytes=64800000
        ),
    )(u, k, e, s, sites, vias, patterns, pattern_currents)


def solution(mesh):
    spec = P(None, "die", "row", "col")
    in_specs = (
        spec,
        spec,
        spec,
        spec,
        P("die", "row", "col", None),
        P(None, "die", "row", "col", None),
        P("die", "row", "col"),
        P(),
    )
    return jax.shard_map(local, mesh=mesh, in_specs=in_specs, out_specs=spec, check_vma=False)
```

```python
import jax
import jax.numpy as jnp
from jax import lax
from jax.experimental import pallas as pl
from jax.experimental.pallas import tpu as pltpu
from jax.sharding import PartitionSpec as P

BS = 16
LANES = 128
VMEM_LIMIT = 64800000
PAD = 8
W1, W2 = 0.85, 1.35
ALPHA = W1 + W2 * (1.0 - W1)
BETA = W1 * W2
MESH = pl.DeviceIdType.MESH
EACH_1, EACH_2 = 8, 8
TILES_STEP, PACK_STEP, FIX_STEP = 2, 4, 4
N_U, N_S, S_U, N_D, S_D = range(5)
f32 = jnp.float32


def kernel(
    u_hbm, k_hbm, e_hbm, s_hbm, site_hbm, via_hbm, pat_hbm, pc_hbm, out,
    us, es, ss, ks, xs, ds, ts, ws, halo,
    sites, vias, pat, pc, tab,
    snd_e, snd_w, col_w, col_e, snd_e2, snd_w2, col_w2, col_e2,
    die_snd, die_rcv, die_snd2, die_rcv2,
    load_sem, small_sem, send_sem, recv_sem,
):
    nets, layers, tiles, rows, _ = es.shape
    octets = rows // 8
    block_rows = rows // BS
    planes = [(n, l) for n in range(nets) for l in range(layers)]
    die, row, col = lax.axis_index("die"), lax.axis_index("row"), lax.axis_index("col")
    n_row, n_col = lax.axis_size("row"), lax.axis_size("col")
    has_n, has_s = row > 0, row < n_row - 1
    has_w, has_e = col > 0, col < n_col - 1
    first_die = die == 0

    barrier = pltpu.get_barrier_semaphore()

    def greet(there, **where):
        @pl.when(there)
        def _():
            pl.semaphore_signal(barrier, inc=1, device_id=where, device_id_type=MESH)

    greet(has_n, row=row - 1)
    greet(has_s, row=row + 1)
    greet(has_w, col=col - 1)
    greet(has_e, col=col + 1)
    pl.semaphore_signal(barrier, inc=1, device_id={"die": 1 - die}, device_id_type=MESH)

    def load(src, dst, pad, c, sem):
        pltpu.make_async_copy(
            src.at[:, :, :, c * LANES : (c + 1) * LANES], dst.at[:, :, c, pad : pad + rows, :], sem
        ).start()

    def loaded(whole, sem):
        pltpu.make_async_copy(whole, whole, sem).wait()

    for c in range(tiles):
        load(u_hbm, us, PAD, c, load_sem.at[0])
    load(e_hbm, es, 0, tiles - 1, load_sem.at[1])
    for c in range(tiles):
        load(s_hbm, ss, PAD, c, load_sem.at[2])
    small = [
        pltpu.make_async_copy(src, dst, small_sem.at[i])
        for i, (src, dst) in enumerate(((site_hbm, sites), (via_hbm, vias), (pat_hbm, pat), (pc_hbm, pc)))
    ]
    for copy in small:
        copy.start()
    for c in range(tiles - 1):
        load(e_hbm, es, 0, c, load_sem.at[3])
    for c in range(tiles):
        load(k_hbm, ks, 0, c, load_sem.at[4])

    last = PAD + rows - 1
    zero_row = jnp.zeros((tiles, LANES), f32)
    for n, l in planes:
        for ref, at in ((us, PAD - 1), (us, PAD + rows), (ss, PAD - 1), (ds, PAD - 1), (ds, PAD + rows)):
            ref[n, l, :, at, :] = zero_row

    def message(i, src, dst, **where):
        return pltpu.make_async_remote_copy(
            src_ref=src,
            dst_ref=dst,
            send_sem=send_sem.at[i],
            recv_sem=recv_sem.at[i],
            device_id=where,
            device_id_type=MESH,
        )

    def line(ref, at):
        return ref.at[:, :, :, at : at + 1, :]

    south_u = message(0, line(us, last), line(halo, N_U), row=row + 1)
    south_s = message(1, line(ss, last), line(halo, N_S), row=row + 1)
    north_u = message(2, line(us, PAD), line(halo, S_U), row=row - 1)
    east_1 = message(3, snd_e, col_w, col=col + 1)
    west_1 = message(4, snd_w, col_e, col=col - 1)
    die_1 = message(5, die_snd, die_rcv, die=1 - die)
    south_d = message(6, line(ds, last), line(halo, N_D), row=row + 1)
    north_d = message(7, line(ds, PAD), line(halo, S_D), row=row - 1)
    east_2 = message(8, snd_e2, col_w2, col=col + 1)
    west_2 = message(9, snd_w2, col_e2, col=col - 1)
    die_2 = message(10, die_snd2, die_rcv2, die=1 - die)

    def on(condition, *actions):
        @pl.when(condition)
        def _():
            for action in actions:
                action()

    def clear(side, *at):
        @pl.when(jnp.logical_not(side))
        def _():
            for n, l in planes:
                for i in at:
                    halo[n, l, :, i, :] = zero_row

    clear(has_n, N_U, N_S, N_D)
    clear(has_s, S_U, S_D)

    def clear_columns(side, *refs):
        @pl.when(jnp.logical_not(side))
        def _():
            for ref in refs:
                ref[...] = jnp.zeros(ref.shape, f32)

    clear_columns(has_w, col_w, col_w2)
    clear_columns(has_e, col_e, col_e2)

    lane = lax.broadcasted_iota(jnp.int32, (8, LANES), 1)
    sub = lax.broadcasted_iota(jnp.int32, (8, LANES), 0)
    low = lane % BS
    group = lane // BS

    loaded(us.at[:, :, :, PAD : PAD + rows, :], load_sem.at[0])
    loaded(es.at[:, :, tiles - 1], load_sem.at[1])

    @pl.when(jnp.logical_not(has_e))
    def _():
        for n, l in planes:
            for o in range(octets):
                at = slice(o * 8, o * 8 + 8)
                es[n, l, tiles - 1, at, :] = jnp.where(lane == LANES - 1, 0.0, es[n, l, tiles - 1, at, :])

    def pack_columns():
        def body(step, _):
            for k in range(PACK_STEP):
                pack(pl.multiple_of(step * (8 * PACK_STEP) + k * 8, 8))
            return 0

        def pack(at):
            to_e = jnp.zeros((8, LANES), f32)
            to_w = jnp.zeros((8, LANES), f32)
            for p, (n, l) in enumerate(planes):
                final = us[n, l, tiles - 1, pl.ds(at + PAD, 8), :]
                to_e = jnp.where(lane == p, pltpu.roll(final, p + 1, 1), to_e)
                first = us[n, l, 0, pl.ds(at + PAD, 8), :]
                to_w = jnp.where(lane == p, pltpu.roll(first, p, 1) if p else first, to_w)
                q = len(planes) + p
                edge = es[n, l, tiles - 1, pl.ds(at, 8), :]
                to_e = jnp.where(lane == q, pltpu.roll(edge, q + 1, 1), to_e)
            snd_e[pl.ds(at, 8), :] = to_e
            snd_w[pl.ds(at, 8), :] = to_w

        lax.fori_loop(0, octets // PACK_STEP, body, 0)

    pack_columns()

    loaded(ss.at[:, :, :, PAD : PAD + rows, :], load_sem.at[2])

    @pl.when(jnp.logical_not(has_s))
    def _():
        for n, l in planes:
            ss[n, l, :, last, :] = zero_row

    neighbours = 1 + sum(jnp.where(there, 1, 0) for there in (has_n, has_s, has_w, has_e))
    pl.semaphore_wait(barrier, neighbours)
    on(has_s, south_u.start, south_s.start)
    on(has_n, north_u.start)
    on(has_e, east_1.start)
    on(has_w, west_1.start)

    for copy in small[:2]:
        copy.wait()
    block_id = jnp.where(low < tiles, sub * (tiles * 8) + low * 8 + group, -1)
    down = [[jnp.zeros((8, LANES), f32) for _ in range(layers)] for _ in range(nets)]
    for l in range(layers):
        for i in range(sites.shape[-1]):
            here = block_id == sites[l, 0, 0, i]
            for n in range(nets):
                down[n][l] = jnp.where(here, vias[n, l, 0, 0, i], down[n][l])

    def centres(pad):
        return pl.ds(pad + BS // 2, block_rows, stride=BS)

    def gather_centres(ref, n, l):
        found = jnp.zeros((8, LANES), f32)
        for c in range(tiles):
            cells = pltpu.roll(ref[n, l, c, centres(PAD), :], (c - BS // 2) % LANES, 1)
            found = jnp.where(low == c, cells, found)
        return found

    def spread(packed, c):
        return jnp.where(low == BS // 2, pltpu.roll(packed, (BS // 2 - c) % LANES, 1), 0.0)

    held = [[gather_centres(us, n, l) for l in range(layers)] for n in range(nets)]
    for n in range(nets):
        die_snd[n] = jnp.where(first_die, held[n][1], held[n][0])
        die_snd[nets + n] = down[n][0]

    die_1.start()

    for copy in small[2:]:
        copy.wait()
    across = sub * BS + low
    patterns = pc.shape[0]

    for i in range(patterns):
        for h in range(2):
            part = jnp.broadcast_to(pc[i : i + 1, h * LANES : (h + 1) * LANES], (8, LANES))
            tab[h, i] = jnp.take_along_axis(part, across, axis=1)

    def currents(step, _):
        per = tiles // TILES_STEP
        l = lax.div(step, per)
        base = lax.rem(step, per) * TILES_STEP
        wide = jnp.concatenate([pat[l], pat[l]], axis=1)
        tables = [[tab[h, i] for i in range(patterns)] for h in range(2)]
        for k in range(TILES_STEP):
            c = base + k
            number = jnp.take_along_axis(wide, c * 8 + group, axis=1)
            for b in range(block_rows):
                mine = jnp.broadcast_to(number[b : b + 1, :], (8, LANES))
                bits = []
                bit = 1
                while bit < patterns:
                    bits.append((mine & bit) != 0)
                    bit *= 2
                for h in range(2):
                    values = tables[h]
                    for odd in bits:
                        values = [
                            jnp.where(odd, values[i + 1], values[i]) for i in range(0, len(values), 2)
                        ]
                    at = b * BS + h * 8
                    xs[l, c, at : at + 8, :] = values[0]
        return 0

    lax.fori_loop(0, layers * tiles // TILES_STEP, currents, 0)

    loaded(es.at[:, :, : tiles - 1], load_sem.at[3])
    loaded(ks, load_sem.at[4])


    def sweep_1(n, l, at):
        here, mid, up, dn = (pl.ds(at + i, 8) for i in (0, PAD, PAD - 1, PAD + 1))

        def fetch(c):
            u, e = us[n, l, c, mid, :], es[n, l, c, here, :]
            return u, e, pltpu.roll(u, LANES - 1, 1), pltpu.roll(u, 1, 1), pltpu.roll(e, 1, 1)

        before, now = (0.0,) * 5, fetch(0)
        for c in range(tiles):
            after = fetch(c + 1) if c + 1 < tiles else (0.0,) * 5
            u, e, u_e, u_w, e_w = now
            u_e = jnp.where(lane == LANES - 1, after[2], u_e)
            u_w = jnp.where(lane == 0, before[3], u_w)
            west = jnp.where(lane == 0, before[4], e_w)
            k, s, s_n = ks[n, l, c, here, :], ss[n, l, c, mid, :], ss[n, l, c, up, :]
            x = xs[l, c, here, :]
            diagonal = (k + e) + (west + s) + s_n
            beside = (e * u_e + west * u_w) + (s * us[n, l, c, dn, :] + s_n * us[n, l, c, up, :])
            rest = k * u + (x if n else -x)
            inverse = 1.0 / diagonal
            ds[n, l, c, mid, :] = (rest + beside) * inverse - u
            ts[n, l, c, here, :] = inverse * BETA
            ws[n, l, c, here, :] = west
            before, now = now, after

    def sweep_2(n, l, at):
        here, mid, up, dn = (pl.ds(at + i, 8) for i in (0, PAD, PAD - 1, PAD + 1))

        def fetch(c):
            d = ds[n, l, c, mid, :]
            return d, pltpu.roll(d, LANES - 1, 1), pltpu.roll(d, 1, 1)

        before, now = (0.0,) * 3, fetch(0)
        for c in range(tiles):
            after = fetch(c + 1) if c + 1 < tiles else (0.0,) * 3
            d, d_e, d_w = now
            d_e = jnp.where(lane == LANES - 1, after[1], d_e)
            d_w = jnp.where(lane == 0, before[2], d_w)
            beside = (es[n, l, c, here, :] * d_e + ws[n, l, c, here, :] * d_w) + (
                ss[n, l, c, mid, :] * ds[n, l, c, dn, :] + ss[n, l, c, up, :] * ds[n, l, c, up, :]
            )
            out[n, l, c, here, :] = (us[n, l, c, mid, :] + ALPHA * d) + ts[n, l, c, here, :] * beside
            before, now = now, after

    def everywhere(sweep, n, each):
        groups = octets // each

        def body(i, _):
            l = lax.div(i, groups)
            base = lax.rem(i, groups) * each
            for k in range(each):
                sweep(n, l, pl.multiple_of((base + k) * 8, 8))
            return 0

        lax.fori_loop(0, layers * groups, body, 0)

    for n in range(nets):
        everywhere(sweep_1, n, EACH_1)

    def turn(v, source, target):
        shift = (target - source) % LANES
        return pltpu.roll(v, shift, 1) if shift else v

    def in_columns(fix):
        def body(step, _):
            for k in range(FIX_STEP):
                at = pl.multiple_of(step * (8 * FIX_STEP) + k * 8, 8)
                for p, (n, l) in enumerate(planes):
                    fix(p, n, l, at)
            return 0

        lax.fori_loop(0, octets // FIX_STEP, body, 0)

    die_1.wait_recv()
    link = [down[n][1] for n in range(nets)]
    outer = [[down[n][0], jnp.where(first_die, die_rcv[nets + n], 0.0)] for n in range(nets)]
    fresh = []
    for n, l in planes:
        beyond = die_rcv[n]
        if l == 0:
            beyond = jnp.where(first_die, 1.0 if n == 0 else 0.0, beyond)
        total = link[n] + outer[n][l]
        pull = link[n] * (held[n][1 - l] - held[n][l]) + outer[n][l] * (beyond - held[n][l])
        for c in range(tiles):
            t = ts[n, l, c, centres(0), :]
            a = t * (1.0 / BETA)
            scale = 1.0 / (1.0 + a * spread(total, c))
            fresh.append(
                (n, l, c, (ds[n, l, c, centres(PAD), :] + a * spread(pull, c)) * scale, t * scale)
            )
    for n, l, c, d, t in fresh:
        ds[n, l, c, centres(PAD), :] = d
        ts[n, l, c, centres(0), :] = t
    moved = [[gather_centres(ds, n, l) for l in range(layers)] for n in range(nets)]
    for n in range(nets):
        die_snd2[n] = jnp.where(first_die, moved[n][1], moved[n][0])

    on(has_n, south_u.wait_recv, south_s.wait_recv)
    on(has_s, north_u.wait_recv)
    fresh = []
    for n, l in planes:
        t, u = ts[n, l, :, 0, :], us[n, l, :, PAD, :]
        part = t * halo[n, l, :, N_S, :] * (1.0 / BETA)
        scale = 1.0 / (1.0 + part)
        gain = ts[n, l, :, rows - 1, :] * ss[n, l, :, last, :] * (1.0 / BETA)
        fresh.append(
            (
                n,
                l,
                (ds[n, l, :, PAD, :] + part * (halo[n, l, :, N_U, :] - u)) * scale,
                t * scale,
                ds[n, l, :, last, :] + gain * halo[n, l, :, S_U, :],
            )
        )
    for n, l, d, t, d_last in fresh:
        ds[n, l, :, PAD, :] = d
        ts[n, l, :, 0, :] = t
        ds[n, l, :, last, :] = d_last

    die_2.start()
    on(has_w, east_1.wait_recv)
    on(has_e, west_1.wait_recv)

    def join_columns(step, _):
        for k in range(FIX_STEP):
            at = pl.multiple_of(step * (8 * FIX_STEP) + k * 8, 8)
            here, mid = pl.ds(at, 8), pl.ds(at + PAD, 8)
            c = tiles - 1
            to_e = jnp.zeros((8, LANES), f32)
            to_w = jnp.zeros((8, LANES), f32)
            from_e, from_w = col_e[here, :], col_w[here, :]
            fresh = []
            for p, (n, l) in enumerate(planes):
                gain = ts[n, l, c, here, :] * es[n, l, c, here, :] * (1.0 / BETA)
                final = ds[n, l, c, mid, :] + jnp.where(
                    lane == LANES - 1, gain * turn(from_e, p, LANES - 1), 0.0
                )
                t, first, u = ts[n, l, 0, here, :], ds[n, l, 0, mid, :], us[n, l, 0, mid, :]
                edge = turn(from_w, len(planes) + p, 0)
                part = jnp.where(lane == 0, t * edge * (1.0 / BETA), 0.0)
                scale = 1.0 / (1.0 + part)
                first = (first + part * (turn(from_w, p, 0) - u)) * scale
                to_e = jnp.where(lane == p, turn(final, LANES - 1, p), to_e)
                to_w = jnp.where(lane == p, turn(first, 0, p), to_w)
                fresh.append((n, l, final, first, t * scale))
            snd_e2[here, :] = to_e
            snd_w2[here, :] = to_w
            for n, l, final, first, t in fresh:
                ds[n, l, c, mid, :] = final
                ds[n, l, 0, mid, :] = first
                ts[n, l, 0, here, :] = t
        return 0

    lax.fori_loop(0, octets // FIX_STEP, join_columns, 0)

    on(has_s, south_d.start)
    on(has_n, north_d.start)
    on(has_e, east_2.start)
    on(has_w, west_2.start)

    for n in range(nets):
        everywhere(sweep_2, n, EACH_2)

    on(has_w, east_2.wait_recv)
    on(has_e, west_2.wait_recv)

    def join_columns_2(p, n, l, at):
        here = pl.ds(at, 8)
        c = tiles - 1
        gain = ts[n, l, c, here, :] * es[n, l, c, here, :]
        final = out[n, l, c, here, :] + jnp.where(
            lane == LANES - 1, gain * turn(col_e2[here, :], p, LANES - 1), 0.0
        )
        edge = turn(col_w[here, :], len(planes) + p, 0)
        first = out[n, l, 0, here, :] + jnp.where(
            lane == 0, ts[n, l, 0, here, :] * edge * turn(col_w2[here, :], p, 0), 0.0
        )
        out[n, l, c, here, :] = final
        out[n, l, 0, here, :] = first

    in_columns(join_columns_2)

    die_2.wait_recv()
    fresh = []
    for n, l in planes:
        reach = outer[n][l] if l else jnp.where(first_die, 0.0, outer[n][l])
        pull = link[n] * moved[n][1 - l] + reach * die_rcv2[n]
        for c in range(tiles):
            value = out[n, l, c, centres(0), :] + ts[n, l, c, centres(0), :] * spread(pull, c)
            fresh.append((n, l, c, value))
    for n, l, c, value in fresh:
        out[n, l, c, centres(0), :] = value

    on(has_n, south_d.wait_recv)
    on(has_s, north_d.wait_recv)
    fresh = []
    for n, l in planes:
        first = ts[n, l, :, 0, :] * halo[n, l, :, N_S, :] * halo[n, l, :, N_D, :]
        final = ts[n, l, :, rows - 1, :] * ss[n, l, :, last, :] * halo[n, l, :, S_D, :]
        fresh.append((n, l, out[n, l, :, 0, :] + first, out[n, l, :, rows - 1, :] + final))
    for n, l, first, final in fresh:
        out[n, l, :, 0, :] = first
        out[n, l, :, rows - 1, :] = final

    on(has_s, south_u.wait_send, south_s.wait_send, south_d.wait_send)
    on(has_n, north_u.wait_send, north_d.wait_send)
    on(has_e, east_1.wait_send, east_2.wait_send)
    on(has_w, west_1.wait_send, west_2.wait_send)
    die_1.wait_send()
    die_2.wait_send()


def store(cells, out, sem):
    nets, layers, tiles, _, _ = cells.shape
    copies = [
        pltpu.make_async_copy(
            cells.at[n, l, c], out.at[n, l, :, c * LANES : (c + 1) * LANES], sem.at[n, l, c]
        )
        for n in range(nets)
        for l in range(layers)
        for c in range(tiles)
    ]
    for copy in copies:
        copy.start()
    for copy in copies:
        copy.wait()


def local(u, k, e, s, sites, vias, patterns, pattern_currents):
    nets, layers, rows, cols = u.shape
    tiles = cols // LANES
    grid = (nets, layers, tiles, rows, LANES)
    padded = (nets, layers, tiles, rows + 2 * PAD, LANES)
    vmem = pltpu.VMEM
    hbm = pl.BlockSpec(memory_space=pltpu.HBM)
    on_chip = pl.BlockSpec(memory_space=vmem)
    column = vmem((rows, LANES), f32)
    packed = vmem((nets, 8, LANES), f32)
    limit = VMEM_LIMIT
    cells = pl.pallas_call(
        kernel,
        out_shape=vmem(grid, f32),
        in_specs=[hbm] * 8,
        out_specs=on_chip,
        scratch_shapes=[
            vmem(padded, f32), vmem(grid, f32), vmem(padded, f32), vmem(grid, f32),
            vmem(grid[1:], f32), vmem(padded, f32), vmem(grid, f32), vmem(grid, f32),
            vmem((nets, layers, tiles, 8, LANES), f32),
            pltpu.SMEM(sites.shape, jnp.int32), pltpu.SMEM(vias.shape, f32),
            vmem(patterns.shape, jnp.int32), vmem(pattern_currents.shape, f32), vmem((2,) + pattern_currents.shape[:1] + (8, LANES), f32),
            column, column, column, column, column, column, column, column,
            vmem((2 * nets, 8, LANES), f32), vmem((2 * nets, 8, LANES), f32), packed, packed,
            pltpu.SemaphoreType.DMA((5,)), pltpu.SemaphoreType.DMA((4,)),
            pltpu.SemaphoreType.DMA((11,)), pltpu.SemaphoreType.DMA((11,)),
        ],
        compiler_params=pltpu.CompilerParams(
            collective_id=0, has_side_effects=True, vmem_limit_bytes=limit
        ),
    )(u, k, e, s, sites, vias, patterns, pattern_currents)
    return pl.pallas_call(
        store,
        out_shape=jax.ShapeDtypeStruct(u.shape, f32),
        in_specs=[on_chip],
        out_specs=hbm,
        scratch_shapes=[pltpu.SemaphoreType.DMA((nets, layers, tiles))],
        compiler_params=pltpu.CompilerParams(vmem_limit_bytes=1024 * 1024),
    )(cells)


def solution(mesh):
    spec = P(None, "die", "row", "col")
    in_specs = (
        spec,
        spec,
        spec,
        spec,
        P("die", "row", "col", None),
        P(None, "die", "row", "col", None),
        P("die", "row", "col"),
        P(),
    )
    return jax.shard_map(local, mesh=mesh, in_specs=in_specs, out_specs=spec, check_vma=False)
```

```python
import jax
import jax.numpy as jnp
from jax import lax
from jax.experimental import pallas as pl
from jax.experimental.pallas import tpu as pltpu
from jax.sharding import PartitionSpec as P

BS = 16
LANES = 128
VMEM_LIMIT = 64800000
PAD = 8
W1, W2 = 0.85, 1.35
ALPHA = W1 + W2 * (1.0 - W1)
BETA = W1 * W2
MESH = pl.DeviceIdType.MESH
EACH_1, EACH_2 = 7, 8
TILES_STEP, PACK_STEP, FIX_STEP, FIX_INSIDE = 2, 4, 4, 7
N_U, N_S, S_U, N_D, S_D, N_T, S_T = range(7)
f32 = jnp.float32


def kernel(
    u_hbm, k_hbm, e_hbm, s_hbm, site_hbm, via_hbm, pat_hbm, pc_hbm, out,
    us, es, ss, ks, xs, ds, ts, ws, halo,
    sites, vias, pat, pc, tab,
    snd_e, snd_w, col_w, col_e, snd_e2, snd_w2, col_w2, col_e2, thin, thin_rcv,
    die_snd, die_rcv, die_snd2, die_rcv2,
    load_sem, small_sem, send_sem, recv_sem,
):
    nets, layers, tiles, rows, _ = es.shape
    octets = rows // 8
    block_rows = rows // BS
    planes = [(n, l) for n in range(nets) for l in range(layers)]
    die, row, col = lax.axis_index("die"), lax.axis_index("row"), lax.axis_index("col")
    n_row, n_col = lax.axis_size("row"), lax.axis_size("col")
    has_n, has_s = row > 0, row < n_row - 1
    has_w, has_e = col > 0, col < n_col - 1
    first_die = die == 0

    barrier = pltpu.get_barrier_semaphore()

    def greet(there, **where):
        @pl.when(there)
        def _():
            pl.semaphore_signal(barrier, inc=1, device_id=where, device_id_type=MESH)

    greet(has_n, row=row - 1)
    greet(has_s, row=row + 1)
    greet(has_w, col=col - 1)
    greet(has_e, col=col + 1)
    pl.semaphore_signal(barrier, inc=1, device_id={"die": 1 - die}, device_id_type=MESH)

    def load(src, dst, pad, c, sem):
        pltpu.make_async_copy(
            src.at[:, :, :, c * LANES : (c + 1) * LANES], dst.at[:, :, c, pad : pad + rows, :], sem
        ).start()

    def loaded(whole, sem):
        pltpu.make_async_copy(whole, whole, sem).wait()

    for c in range(tiles):
        load(u_hbm, us, PAD, c, load_sem.at[0])
    for c in range(tiles):
        load(s_hbm, ss, PAD, c, load_sem.at[2])
    load(e_hbm, es, 0, tiles - 1, load_sem.at[1])
    small = [
        pltpu.make_async_copy(src, dst, small_sem.at[i])
        for i, (src, dst) in enumerate(((site_hbm, sites), (via_hbm, vias), (pat_hbm, pat), (pc_hbm, pc)))
    ]
    for copy in small:
        copy.start()
    for c in range(tiles - 1):
        load(e_hbm, es, 0, c, load_sem.at[3])
    for c in range(tiles):
        load(k_hbm, ks, 0, c, load_sem.at[4])

    last = PAD + rows - 1
    zero_row = jnp.zeros((tiles, LANES), f32)
    for n, l in planes:
        for ref, at in ((us, PAD - 1), (us, PAD + rows), (ss, PAD - 1), (ds, PAD - 1), (ds, PAD + rows)):
            ref[n, l, :, at, :] = zero_row

    def message(i, src, dst, **where):
        return pltpu.make_async_remote_copy(
            src_ref=src,
            dst_ref=dst,
            send_sem=send_sem.at[i],
            recv_sem=recv_sem.at[i],
            device_id=where,
            device_id_type=MESH,
        )

    def line(ref, at):
        return ref.at[:, :, :, at : at + 1, :]

    south_u = message(0, line(us, last), line(halo, N_U), row=row + 1)
    south_s = message(1, line(ss, last), line(halo, N_S), row=row + 1)
    north_u = message(2, line(us, PAD), line(halo, S_U), row=row - 1)
    east_1 = message(3, thin.at[0], thin_rcv.at[0], col=col + 1)
    west_1 = message(4, thin.at[1], thin_rcv.at[1], col=col - 1)
    die_1 = message(5, die_snd, die_rcv, die=1 - die)
    south_d = message(6, line(ds, last), line(halo, N_D), row=row + 1)
    north_d = message(7, line(ds, PAD), line(halo, S_D), row=row - 1)
    east_2 = message(8, thin.at[2], thin_rcv.at[2], col=col + 1)
    west_2 = message(9, thin.at[3], thin_rcv.at[3], col=col - 1)
    south_t = message(11, line(ts, rows - 1), line(halo, N_T), row=row + 1)
    north_t = message(12, line(ts, 0), line(halo, S_T), row=row - 1)
    die_2 = message(10, die_snd2, die_rcv2, die=1 - die)

    def on(condition, *actions):
        @pl.when(condition)
        def _():
            for action in actions:
                action()

    def clear(side, *at):
        @pl.when(jnp.logical_not(side))
        def _():
            for n, l in planes:
                for i in at:
                    halo[n, l, :, i, :] = zero_row

    clear(has_n, N_U, N_S, N_D, N_T)
    clear(has_s, S_U, S_D, S_T)

    def clear_columns(side, *slots):
        @pl.when(jnp.logical_not(side))
        def _():
            for i in slots:
                thin_rcv[i] = jnp.zeros(thin_rcv.shape[1:], f32)

    clear_columns(has_w, 0, 2)
    clear_columns(has_e, 1, 3)

    def make_thin(i, ref):
        thin[i] = jnp.transpose(ref[...])[: thin.shape[1]]

    def make_wide(i, ref):
        few = thin_rcv[i]
        rest = jnp.zeros((LANES - few.shape[0], LANES), f32)
        ref[...] = jnp.transpose(jnp.concatenate([few, rest], axis=0))

    lane = lax.broadcasted_iota(jnp.int32, (8, LANES), 1)
    sub = lax.broadcasted_iota(jnp.int32, (8, LANES), 0)
    low = lane % BS
    group = lane // BS

    for copy in small[:2]:
        copy.wait()
    block_id = jnp.where(low < tiles, sub * (tiles * 8) + low * 8 + group, -1)
    down = [[jnp.zeros((8, LANES), f32) for _ in range(layers)] for _ in range(nets)]
    for l in range(layers):
        for i in range(sites.shape[-1]):
            here = block_id == sites[l, 0, 0, i]
            for n in range(nets):
                down[n][l] = jnp.where(here, vias[n, l, 0, 0, i], down[n][l])

    for copy in small[2:]:
        copy.wait()
    across = sub * BS + low
    patterns = pc.shape[0]

    for i in range(patterns):
        for h in range(2):
            part = jnp.broadcast_to(pc[i : i + 1, h * LANES : (h + 1) * LANES], (8, LANES))
            tab[h, i] = jnp.take_along_axis(part, across, axis=1)

    def pack_columns():
        def body(step, _):
            for k in range(PACK_STEP):
                pack(pl.multiple_of(step * (8 * PACK_STEP) + k * 8, 8))
            return 0

        def pack(at):
            to_e = jnp.zeros((8, LANES), f32)
            to_w = jnp.zeros((8, LANES), f32)
            for p, (n, l) in enumerate(planes):
                final = us[n, l, tiles - 1, pl.ds(at + PAD, 8), :]
                to_e = jnp.where(lane == p, pltpu.roll(final, p + 1, 1), to_e)
                first = us[n, l, 0, pl.ds(at + PAD, 8), :]
                to_w = jnp.where(lane == p, pltpu.roll(first, p, 1) if p else first, to_w)
                q = len(planes) + p
                edge = es[n, l, tiles - 1, pl.ds(at, 8), :]
                to_e = jnp.where(lane == q, pltpu.roll(edge, q + 1, 1), to_e)
            snd_e[pl.ds(at, 8), :] = to_e
            snd_w[pl.ds(at, 8), :] = to_w

        lax.fori_loop(0, octets // PACK_STEP, body, 0)

    loaded(us.at[:, :, :, PAD : PAD + rows, :], load_sem.at[0])
    loaded(ss.at[:, :, :, PAD : PAD + rows, :], load_sem.at[2])

    @pl.when(jnp.logical_not(has_s))
    def _():
        for n, l in planes:
            ss[n, l, :, last, :] = zero_row

    neighbours = 1 + sum(jnp.where(there, 1, 0) for there in (has_n, has_s, has_w, has_e))
    pl.semaphore_wait(barrier, neighbours)
    on(has_s, south_u.start, south_s.start)
    on(has_n, north_u.start)
    loaded(es.at[:, :, tiles - 1], load_sem.at[1])

    @pl.when(jnp.logical_not(has_e))
    def _():
        for n, l in planes:
            for o in range(octets):
                at = slice(o * 8, o * 8 + 8)
                es[n, l, tiles - 1, at, :] = jnp.where(lane == LANES - 1, 0.0, es[n, l, tiles - 1, at, :])

    pack_columns()
    make_thin(0, snd_e)
    make_thin(1, snd_w)
    on(has_e, east_1.start)
    on(has_w, west_1.start)

    def centres(pad):
        return pl.ds(pad + BS // 2, block_rows, stride=BS)

    def gather_centres(ref, n, l):
        found = jnp.zeros((8, LANES), f32)
        for c in range(tiles):
            cells = pltpu.roll(ref[n, l, c, centres(PAD), :], (c - BS // 2) % LANES, 1)
            found = jnp.where(low == c, cells, found)
        return found

    def spread(packed, c):
        return jnp.where(low == BS // 2, pltpu.roll(packed, (BS // 2 - c) % LANES, 1), 0.0)

    held = [[gather_centres(us, n, l) for l in range(layers)] for n in range(nets)]
    for n in range(nets):
        die_snd[n] = jnp.where(first_die, held[n][1], held[n][0])
        die_snd[nets + n] = down[n][0]

    die_1.start()

    def currents(step, _):
        per = tiles // TILES_STEP
        l = lax.div(step, per)
        base = lax.rem(step, per) * TILES_STEP
        wide = jnp.concatenate([pat[l], pat[l]], axis=1)
        tables = [[tab[h, i] for i in range(patterns)] for h in range(2)]
        for k in range(TILES_STEP):
            c = base + k
            number = jnp.take_along_axis(wide, c * 8 + group, axis=1)
            for b in range(block_rows):
                mine = jnp.broadcast_to(number[b : b + 1, :], (8, LANES))
                bits = []
                bit = 1
                while bit < patterns:
                    bits.append((mine & bit) != 0)
                    bit *= 2
                for h in range(2):
                    values = tables[h]
                    for odd in bits:
                        values = [
                            jnp.where(odd, values[i + 1], values[i]) for i in range(0, len(values), 2)
                        ]
                    at = b * BS + h * 8
                    xs[l, c, at : at + 8, :] = values[0]
        return 0

    lax.fori_loop(0, layers * tiles // TILES_STEP, currents, 0)

    loaded(es.at[:, :, : tiles - 1], load_sem.at[3])
    loaded(ks, load_sem.at[4])


    def sweep_1(n, l, at):
        here, mid, up, dn = (pl.ds(at + i, 8) for i in (0, PAD, PAD - 1, PAD + 1))

        def fetch(c):
            u, e = us[n, l, c, mid, :], es[n, l, c, here, :]
            return u, e, pltpu.roll(u, LANES - 1, 1), pltpu.roll(u, 1, 1), pltpu.roll(e, 1, 1)

        before, now = (0.0,) * 5, fetch(0)
        for c in range(tiles):
            after = fetch(c + 1) if c + 1 < tiles else (0.0,) * 5
            u, e, u_e, u_w, e_w = now
            u_e = jnp.where(lane == LANES - 1, after[2], u_e)
            u_w = jnp.where(lane == 0, before[3], u_w)
            west = jnp.where(lane == 0, before[4], e_w)
            k, s, s_n = ks[n, l, c, here, :], ss[n, l, c, mid, :], ss[n, l, c, up, :]
            x = xs[l, c, here, :]
            diagonal = (k + e) + (west + s) + s_n
            beside = (e * u_e + west * u_w) + (s * us[n, l, c, dn, :] + s_n * us[n, l, c, up, :])
            rest = k * u + (x if n else -x)
            inverse = 1.0 / diagonal
            ds[n, l, c, mid, :] = (rest + beside) * inverse - u
            ts[n, l, c, here, :] = inverse * BETA
            ws[n, l, c, here, :] = west
            before, now = now, after

    def sweep_2(n, l, at):
        here, mid, up, dn = (pl.ds(at + i, 8) for i in (0, PAD, PAD - 1, PAD + 1))

        def fetch(c):
            d = ds[n, l, c, mid, :]
            return d, pltpu.roll(d, LANES - 1, 1), pltpu.roll(d, 1, 1)

        before, now = (0.0,) * 3, fetch(0)
        for c in range(tiles):
            after = fetch(c + 1) if c + 1 < tiles else (0.0,) * 3
            d, d_e, d_w = now
            d_e = jnp.where(lane == LANES - 1, after[1], d_e)
            d_w = jnp.where(lane == 0, before[2], d_w)
            beside = (es[n, l, c, here, :] * d_e + ws[n, l, c, here, :] * d_w) + (
                ss[n, l, c, mid, :] * ds[n, l, c, dn, :] + ss[n, l, c, up, :] * ds[n, l, c, up, :]
            )
            out[n, l, c, here, :] = (us[n, l, c, mid, :] + ALPHA * d) + ts[n, l, c, here, :] * beside
            before, now = now, after

    def over(sweep, n, first, each, groups):
        def body(i, _):
            l = lax.div(i, groups)
            base = first + lax.rem(i, groups) * each
            for k in range(each):
                sweep(n, l, pl.multiple_of((base + k) * 8, 8))
            return 0

        lax.fori_loop(0, layers * groups, body, 0)

    def ends(n):
        def body(l, _):
            for o in (0, octets - 1):
                sweep_1(n, l, o * 8)
            return 0

        lax.fori_loop(0, layers, body, 0)

    for n in range(nets):
        ends(n)

    def turn(v, source, target):
        shift = (target - source) % LANES
        return pltpu.roll(v, shift, 1) if shift else v

    def in_columns(fix):
        def body(step, _):
            for k in range(FIX_STEP):
                at = pl.multiple_of(step * (8 * FIX_STEP) + k * 8, 8)
                for p, (n, l) in enumerate(planes):
                    fix(p, n, l, at)
            return 0

        lax.fori_loop(0, octets // FIX_STEP, body, 0)

    on(has_w, east_1.wait_recv)
    on(has_e, west_1.wait_recv)
    make_wide(0, col_w)
    make_wide(1, col_e)

    def join_columns(at, send):
        here, mid = pl.ds(at, 8), pl.ds(at + PAD, 8)
        c = tiles - 1
        to_e = jnp.zeros((8, LANES), f32)
        to_w = jnp.zeros((8, LANES), f32)
        from_e, from_w = col_e[here, :], col_w[here, :]
        fresh = []
        for p, (n, l) in enumerate(planes):
            gain = ts[n, l, c, here, :] * es[n, l, c, here, :] * (1.0 / BETA)
            final = ds[n, l, c, mid, :] + jnp.where(
                lane == LANES - 1, gain * turn(from_e, p, LANES - 1), 0.0
            )
            t, first, u = ts[n, l, 0, here, :], ds[n, l, 0, mid, :], us[n, l, 0, mid, :]
            edge = turn(from_w, len(planes) + p, 0)
            part = jnp.where(lane == 0, t * edge * (1.0 / BETA), 0.0)
            scale = 1.0 / (1.0 + part)
            first = (first + part * (turn(from_w, p, 0) - u)) * scale
            if send:
                to_e = jnp.where(lane == p, turn(final, LANES - 1, p), to_e)
                to_w = jnp.where(lane == p, turn(first, 0, p), to_w)
            fresh.append((n, l, final, first, t * scale))
        if send:
            snd_e2[here, :] = to_e
            snd_w2[here, :] = to_w
        for n, l, final, first, t in fresh:
            ds[n, l, c, mid, :] = final
            ds[n, l, 0, mid, :] = first
            ts[n, l, 0, here, :] = t

    for o in (0, octets - 1):
        join_columns(o * 8, False)
    on(has_s, south_d.start, south_t.start)
    on(has_n, north_d.start, north_t.start)

    for n in range(nets):
        over(sweep_1, n, 1, EACH_1, (octets - 2) // EACH_1)

    def join_inside(step, _):
        for k in range(FIX_INSIDE):
            join_columns(pl.multiple_of((1 + step * FIX_INSIDE + k) * 8, 8), True)
        return 0

    lax.fori_loop(0, (octets - 2) // FIX_INSIDE, join_inside, 0)

    die_1.wait_recv()
    link = [down[n][1] for n in range(nets)]
    outer = [[down[n][0], jnp.where(first_die, die_rcv[nets + n], 0.0)] for n in range(nets)]
    fresh = []
    for n, l in planes:
        beyond = die_rcv[n]
        if l == 0:
            beyond = jnp.where(first_die, 1.0 if n == 0 else 0.0, beyond)
        total = link[n] + outer[n][l]
        pull = link[n] * (held[n][1 - l] - held[n][l]) + outer[n][l] * (beyond - held[n][l])
        for c in range(tiles):
            t = ts[n, l, c, centres(0), :]
            a = t * (1.0 / BETA)
            scale = 1.0 / (1.0 + a * spread(total, c))
            fresh.append(
                (n, l, c, (ds[n, l, c, centres(PAD), :] + a * spread(pull, c)) * scale, t * scale)
            )
    for n, l, c, d, t in fresh:
        ds[n, l, c, centres(PAD), :] = d
        ts[n, l, c, centres(0), :] = t
    moved = [[gather_centres(ds, n, l) for l in range(layers)] for n in range(nets)]
    for n in range(nets):
        die_snd2[n] = jnp.where(first_die, moved[n][1], moved[n][0])

    die_2.start()

    on(has_n, south_u.wait_recv, south_s.wait_recv)
    on(has_s, north_u.wait_recv)
    on(has_s, south_d.wait_send, south_t.wait_send)
    on(has_n, north_d.wait_send, north_t.wait_send)
    fresh = []
    for n, l in planes:
        t, u = ts[n, l, :, 0, :], us[n, l, :, PAD, :]
        part = t * halo[n, l, :, N_S, :] * (1.0 / BETA)
        scale = 1.0 / (1.0 + part)
        gain = ts[n, l, :, rows - 1, :] * ss[n, l, :, last, :] * (1.0 / BETA)
        fresh.append(
            (
                n,
                l,
                (ds[n, l, :, PAD, :] + part * (halo[n, l, :, N_U, :] - u)) * scale,
                t * scale,
                ds[n, l, :, last, :] + gain * halo[n, l, :, S_U, :],
            )
        )
    for n, l, d, t, d_last in fresh:
        ds[n, l, :, PAD, :] = d
        ts[n, l, :, 0, :] = t
        ds[n, l, :, last, :] = d_last

    for o in (0, octets - 1):
        here, mid = slice(o * 8, o * 8 + 8), slice(o * 8 + PAD, o * 8 + PAD + 8)
        to_e = jnp.zeros((8, LANES), f32)
        to_w = jnp.zeros((8, LANES), f32)
        for p, (n, l) in enumerate(planes):
            to_e = jnp.where(lane == p, turn(ds[n, l, tiles - 1, mid, :], LANES - 1, p), to_e)
            to_w = jnp.where(lane == p, turn(ds[n, l, 0, mid, :], 0, p), to_w)
        snd_e2[here, :] = to_e
        snd_w2[here, :] = to_w
    make_thin(2, snd_e2)
    make_thin(3, snd_w2)
    on(has_e, east_2.start)
    on(has_w, west_2.start)

    for n in range(nets):
        over(sweep_2, n, 0, EACH_2, octets // EACH_2)

    on(has_w, east_2.wait_recv)
    on(has_e, west_2.wait_recv)
    make_wide(2, col_w2)
    make_wide(3, col_e2)

    def join_columns_2(p, n, l, at):
        here = pl.ds(at, 8)
        c = tiles - 1
        gain = ts[n, l, c, here, :] * es[n, l, c, here, :]
        final = out[n, l, c, here, :] + jnp.where(
            lane == LANES - 1, gain * turn(col_e2[here, :], p, LANES - 1), 0.0
        )
        edge = turn(col_w[here, :], len(planes) + p, 0)
        first = out[n, l, 0, here, :] + jnp.where(
            lane == 0, ts[n, l, 0, here, :] * edge * turn(col_w2[here, :], p, 0), 0.0
        )
        out[n, l, c, here, :] = final
        out[n, l, 0, here, :] = first

    in_columns(join_columns_2)

    die_2.wait_recv()
    fresh = []
    for n, l in planes:
        reach = outer[n][l] if l else jnp.where(first_die, 0.0, outer[n][l])
        pull = link[n] * moved[n][1 - l] + reach * die_rcv2[n]
        for c in range(tiles):
            value = out[n, l, c, centres(0), :] + ts[n, l, c, centres(0), :] * spread(pull, c)
            fresh.append((n, l, c, value))
    for n, l, c, value in fresh:
        out[n, l, c, centres(0), :] = value

    on(has_n, south_d.wait_recv, south_t.wait_recv)
    on(has_s, north_d.wait_recv, north_t.wait_recv)
    fresh = []
    for n, l in planes:
        north, south = halo[n, l, :, N_S, :], ss[n, l, :, last, :]
        d_n = halo[n, l, :, N_D, :] + halo[n, l, :, N_T, :] * (1.0 / BETA) * north * us[n, l, :, PAD, :]
        part = halo[n, l, :, S_T, :] * (1.0 / BETA) * south
        d_s = (halo[n, l, :, S_D, :] + part * (us[n, l, :, last, :] - halo[n, l, :, S_U, :])) / (
            1.0 + part
        )
        first = ts[n, l, :, 0, :] * north * d_n
        final = ts[n, l, :, rows - 1, :] * south * d_s
        fresh.append((n, l, out[n, l, :, 0, :] + first, out[n, l, :, rows - 1, :] + final))
    for n, l, first, final in fresh:
        out[n, l, :, 0, :] = first
        out[n, l, :, rows - 1, :] = final

    on(has_s, south_u.wait_send, south_s.wait_send)
    on(has_n, north_u.wait_send)
    on(has_e, east_1.wait_send, east_2.wait_send)
    on(has_w, west_1.wait_send, west_2.wait_send)
    die_1.wait_send()
    die_2.wait_send()


def store(cells, out, sem):
    nets, layers, tiles, _, _ = cells.shape
    copies = [
        pltpu.make_async_copy(
            cells.at[n, l, c], out.at[n, l, :, c * LANES : (c + 1) * LANES], sem.at[n, l, c]
        )
        for n in range(nets)
        for l in range(layers)
        for c in range(tiles)
    ]
    for copy in copies:
        copy.start()
    for copy in copies:
        copy.wait()


def local(u, k, e, s, sites, vias, patterns, pattern_currents):
    nets, layers, rows, cols = u.shape
    tiles = cols // LANES
    grid = (nets, layers, tiles, rows, LANES)
    padded = (nets, layers, tiles, rows + 2 * PAD, LANES)
    vmem = pltpu.VMEM
    hbm = pl.BlockSpec(memory_space=pltpu.HBM)
    on_chip = pl.BlockSpec(memory_space=vmem)
    column = vmem((rows, LANES), f32)
    packed = vmem((nets, 8, LANES), f32)
    limit = VMEM_LIMIT
    cells = pl.pallas_call(
        kernel,
        out_shape=vmem(grid, f32),
        in_specs=[hbm] * 8,
        out_specs=on_chip,
        scratch_shapes=[
            vmem(padded, f32), vmem(grid, f32), vmem(padded, f32), vmem(grid, f32),
            vmem(grid[1:], f32), vmem(padded, f32), vmem(grid, f32), vmem(grid, f32),
            vmem((nets, layers, tiles, 8, LANES), f32),
            pltpu.SMEM(sites.shape, jnp.int32), pltpu.SMEM(vias.shape, f32),
            vmem(patterns.shape, jnp.int32), vmem(pattern_currents.shape, f32), vmem((2,) + pattern_currents.shape[:1] + (8, LANES), f32),
            column, column, column, column, column, column, column, column,
            vmem((4, 16, LANES), f32), vmem((4, 16, LANES), f32),
            vmem((2 * nets, 8, LANES), f32), vmem((2 * nets, 8, LANES), f32), packed, packed,
            pltpu.SemaphoreType.DMA((5,)), pltpu.SemaphoreType.DMA((4,)),
            pltpu.SemaphoreType.DMA((13,)), pltpu.SemaphoreType.DMA((13,)),
        ],
        compiler_params=pltpu.CompilerParams(
            collective_id=0, has_side_effects=True, vmem_limit_bytes=limit
        ),
    )(u, k, e, s, sites, vias, patterns, pattern_currents)
    return pl.pallas_call(
        store,
        out_shape=jax.ShapeDtypeStruct(u.shape, f32),
        in_specs=[on_chip],
        out_specs=hbm,
        scratch_shapes=[pltpu.SemaphoreType.DMA((nets, layers, tiles))],
        compiler_params=pltpu.CompilerParams(vmem_limit_bytes=1024 * 1024),
    )(cells)


def solution(mesh):
    spec = P(None, "die", "row", "col")
    in_specs = (
        spec,
        spec,
        spec,
        spec,
        P("die", "row", "col", None),
        P(None, "die", "row", "col", None),
        P("die", "row", "col"),
        P(),
    )
    return jax.shard_map(local, mesh=mesh, in_specs=in_specs, out_specs=spec, check_vma=False)
```

```python
import jax
import jax.numpy as jnp
from jax import lax
from jax.experimental import pallas as pl
from jax.experimental.pallas import tpu as pltpu
from jax.sharding import PartitionSpec as P

BS = 16
LANES = 128
VMEM_LIMIT = 64800000
PAD = 8
W1, W2 = 0.85, 1.35
ALPHA = W1 + W2 * (1.0 - W1)
BETA = W1 * W2
MESH = pl.DeviceIdType.MESH
EACH_1, EACH_2 = 7, 8
TILES_STEP, PACK_STEP, FIX_STEP, FIX_INSIDE = 2, 4, 4, 7
N_U, N_S, S_U, N_D, S_D, N_T, S_T = range(7)
f32 = jnp.float32


def kernel(
    u_hbm, k_hbm, e_hbm, s_hbm, site_hbm, via_hbm, pat_hbm, pc_hbm, out,
    us, es, ss, ks, xs, ds, ts, ws, halo,
    sites, vias, pat, pc, tab,
    snd_e, snd_w, col_w, col_e, snd_e2, snd_w2, col_w2, col_e2, thin, thin_rcv,
    die_snd, die_rcv, die_snd2, die_rcv2,
    load_sem, small_sem, send_sem, recv_sem,
):
    nets, layers, tiles, rows, _ = es.shape
    octets = rows // 8
    block_rows = rows // BS
    planes = [(n, l) for n in range(nets) for l in range(layers)]
    die, row, col = lax.axis_index("die"), lax.axis_index("row"), lax.axis_index("col")
    n_row, n_col = lax.axis_size("row"), lax.axis_size("col")
    has_n, has_s = row > 0, row < n_row - 1
    has_w, has_e = col > 0, col < n_col - 1
    first_die = die == 0

    barrier = pltpu.get_barrier_semaphore()

    def greet(there, **where):
        @pl.when(there)
        def _():
            pl.semaphore_signal(barrier, inc=1, device_id=where, device_id_type=MESH)

    greet(has_n, row=row - 1)
    greet(has_s, row=row + 1)
    greet(has_w, col=col - 1)
    greet(has_e, col=col + 1)
    pl.semaphore_signal(barrier, inc=1, device_id={"die": 1 - die}, device_id_type=MESH)

    def load(src, dst, pad, c, sem):
        pltpu.make_async_copy(
            src.at[:, :, :, c * LANES : (c + 1) * LANES], dst.at[:, :, c, pad : pad + rows, :], sem
        ).start()

    def loaded(whole, sem):
        pltpu.make_async_copy(whole, whole, sem).wait()

    for c in range(tiles):
        load(u_hbm, us, PAD, c, load_sem.at[0])
    for c in range(tiles):
        load(s_hbm, ss, PAD, c, load_sem.at[2])
    load(e_hbm, es, 0, tiles - 1, load_sem.at[1])
    small = [
        pltpu.make_async_copy(src, dst, small_sem.at[i])
        for i, (src, dst) in enumerate(((site_hbm, sites), (via_hbm, vias), (pat_hbm, pat), (pc_hbm, pc)))
    ]
    for copy in small:
        copy.start()
    for c in range(tiles - 1):
        load(e_hbm, es, 0, c, load_sem.at[3])
    for c in range(tiles):
        load(k_hbm, ks, 0, c, load_sem.at[4])

    last = PAD + rows - 1
    zero_row = jnp.zeros((tiles, LANES), f32)
    for n, l in planes:
        for ref, at in ((us, PAD - 1), (us, PAD + rows), (ss, PAD - 1), (ds, PAD - 1), (ds, PAD + rows)):
            ref[n, l, :, at, :] = zero_row

    def message(i, src, dst, **where):
        return pltpu.make_async_remote_copy(
            src_ref=src,
            dst_ref=dst,
            send_sem=send_sem.at[i],
            recv_sem=recv_sem.at[i],
            device_id=where,
            device_id_type=MESH,
        )

    def line(ref, at):
        return ref.at[:, :, :, at : at + 1, :]

    south_u = message(0, line(us, last), line(halo, N_U), row=row + 1)
    south_s = message(1, line(ss, last), line(halo, N_S), row=row + 1)
    north_u = message(2, line(us, PAD), line(halo, S_U), row=row - 1)
    east_1 = message(3, thin.at[0], thin_rcv.at[0], col=col + 1)
    west_1 = message(4, thin.at[1], thin_rcv.at[1], col=col - 1)
    die_1 = message(5, die_snd, die_rcv, die=1 - die)
    south_d = message(6, line(ds, last), line(halo, N_D), row=row + 1)
    north_d = message(7, line(ds, PAD), line(halo, S_D), row=row - 1)
    east_2 = message(8, thin.at[2], thin_rcv.at[2], col=col + 1)
    west_2 = message(9, thin.at[3], thin_rcv.at[3], col=col - 1)
    south_t = message(11, line(ts, rows - 1), line(halo, N_T), row=row + 1)
    north_t = message(12, line(ts, 0), line(halo, S_T), row=row - 1)
    die_2 = message(10, die_snd2, die_rcv2, die=1 - die)

    def on(condition, *actions):
        @pl.when(condition)
        def _():
            for action in actions:
                action()

    def clear(side, *at):
        @pl.when(jnp.logical_not(side))
        def _():
            for n, l in planes:
                for i in at:
                    halo[n, l, :, i, :] = zero_row

    clear(has_n, N_U, N_S, N_D, N_T)
    clear(has_s, S_U, S_D, S_T)

    def clear_columns(side, *slots):
        @pl.when(jnp.logical_not(side))
        def _():
            for i in slots:
                thin_rcv[i] = jnp.zeros(thin_rcv.shape[1:], f32)

    clear_columns(has_w, 0, 2)
    clear_columns(has_e, 1, 3)

    def make_thin(i, ref):
        thin[i] = jnp.transpose(ref[...])[: thin.shape[1]]

    def make_wide(i, ref):
        few = thin_rcv[i]
        rest = jnp.zeros((LANES - few.shape[0], LANES), f32)
        ref[...] = jnp.transpose(jnp.concatenate([few, rest], axis=0))

    lane = lax.broadcasted_iota(jnp.int32, (8, LANES), 1)
    sub = lax.broadcasted_iota(jnp.int32, (8, LANES), 0)
    low = lane % BS
    group = lane // BS

    for copy in small[:2]:
        copy.wait()
    block_id = jnp.where(low < tiles, sub * (tiles * 8) + low * 8 + group, -1)
    down = [[jnp.zeros((8, LANES), f32) for _ in range(layers)] for _ in range(nets)]
    for l in range(layers):
        for i in range(sites.shape[-1]):
            here = block_id == sites[l, 0, 0, i]
            for n in range(nets):
                down[n][l] = jnp.where(here, vias[n, l, 0, 0, i], down[n][l])

    for copy in small[2:]:
        copy.wait()
    across = sub * BS + low
    patterns = pc.shape[0]

    for i in range(patterns):
        for h in range(2):
            part = jnp.broadcast_to(pc[i : i + 1, h * LANES : (h + 1) * LANES], (8, LANES))
            tab[h, i] = jnp.take_along_axis(part, across, axis=1)

    def pack_columns():
        def body(step, _):
            for k in range(PACK_STEP):
                pack(pl.multiple_of(step * (8 * PACK_STEP) + k * 8, 8))
            return 0

        def pack(at):
            to_e = jnp.zeros((8, LANES), f32)
            to_w = jnp.zeros((8, LANES), f32)
            for p, (n, l) in enumerate(planes):
                final = us[n, l, tiles - 1, pl.ds(at + PAD, 8), :]
                to_e = jnp.where(lane == p, pltpu.roll(final, p + 1, 1), to_e)
                first = us[n, l, 0, pl.ds(at + PAD, 8), :]
                to_w = jnp.where(lane == p, pltpu.roll(first, p, 1) if p else first, to_w)
                q = len(planes) + p
                edge = es[n, l, tiles - 1, pl.ds(at, 8), :]
                to_e = jnp.where(lane == q, pltpu.roll(edge, q + 1, 1), to_e)
            snd_e[pl.ds(at, 8), :] = to_e
            snd_w[pl.ds(at, 8), :] = to_w

        lax.fori_loop(0, octets // PACK_STEP, body, 0)

    loaded(us.at[:, :, :, PAD : PAD + rows, :], load_sem.at[0])
    loaded(ss.at[:, :, :, PAD : PAD + rows, :], load_sem.at[2])

    @pl.when(jnp.logical_not(has_s))
    def _():
        for n, l in planes:
            ss[n, l, :, last, :] = zero_row

    neighbours = 1 + sum(jnp.where(there, 1, 0) for there in (has_n, has_s, has_w, has_e))
    pl.semaphore_wait(barrier, neighbours)
    on(has_s, south_u.start, south_s.start)
    on(has_n, north_u.start)
    loaded(es.at[:, :, tiles - 1], load_sem.at[1])

    @pl.when(jnp.logical_not(has_e))
    def _():
        for n, l in planes:
            for o in range(octets):
                at = slice(o * 8, o * 8 + 8)
                es[n, l, tiles - 1, at, :] = jnp.where(lane == LANES - 1, 0.0, es[n, l, tiles - 1, at, :])

    pack_columns()
    make_thin(0, snd_e)
    make_thin(1, snd_w)
    on(has_e, east_1.start)
    on(has_w, west_1.start)

    def centres(pad):
        return pl.ds(pad + BS // 2, block_rows, stride=BS)

    def gather_centres(ref, n, l):
        found = jnp.zeros((8, LANES), f32)
        for c in range(tiles):
            cells = pltpu.roll(ref[n, l, c, centres(PAD), :], (c - BS // 2) % LANES, 1)
            found = jnp.where(low == c, cells, found)
        return found

    def spread(packed, c):
        return jnp.where(low == BS // 2, pltpu.roll(packed, (BS // 2 - c) % LANES, 1), 0.0)

    held = [[gather_centres(us, n, l) for l in range(layers)] for n in range(nets)]
    for n in range(nets):
        die_snd[n] = jnp.where(first_die, held[n][1], held[n][0])
        die_snd[nets + n] = down[n][0]

    die_1.start()

    def currents(step, _):
        per = tiles // TILES_STEP
        l = lax.div(step, per)
        base = lax.rem(step, per) * TILES_STEP
        wide = jnp.concatenate([pat[l], pat[l]], axis=1)
        tables = [[tab[h, i] for i in range(patterns)] for h in range(2)]
        for k in range(TILES_STEP):
            c = base + k
            number = jnp.take_along_axis(wide, c * 8 + group, axis=1)
            for b in range(block_rows):
                mine = jnp.broadcast_to(number[b : b + 1, :], (8, LANES))
                bits = []
                bit = 1
                while bit < patterns:
                    bits.append((mine & bit) != 0)
                    bit *= 2
                for h in range(2):
                    values = tables[h]
                    for odd in bits:
                        values = [
                            jnp.where(odd, values[i + 1], values[i]) for i in range(0, len(values), 2)
                        ]
                    at = b * BS + h * 8
                    xs[l, c, at : at + 8, :] = values[0]
        return 0

    lax.fori_loop(0, layers * tiles // TILES_STEP, currents, 0)

    loaded(es.at[:, :, : tiles - 1], load_sem.at[3])
    loaded(ks, load_sem.at[4])


    def sweep_1(n, l, at):
        here, mid, up, dn = (pl.ds(at + i, 8) for i in (0, PAD, PAD - 1, PAD + 1))

        def fetch(c):
            u, e = us[n, l, c, mid, :], es[n, l, c, here, :]
            return u, e, pltpu.roll(u, LANES - 1, 1), pltpu.roll(u, 1, 1), pltpu.roll(e, 1, 1)

        before, now = (0.0,) * 5, fetch(0)
        for c in range(tiles):
            after = fetch(c + 1) if c + 1 < tiles else (0.0,) * 5
            u, e, u_e, u_w, e_w = now
            u_e = jnp.where(lane == LANES - 1, after[2], u_e)
            u_w = jnp.where(lane == 0, before[3], u_w)
            west = jnp.where(lane == 0, before[4], e_w)
            k, s, s_n = ks[n, l, c, here, :], ss[n, l, c, mid, :], ss[n, l, c, up, :]
            x = xs[l, c, here, :]
            diagonal = (k + e) + (west + s) + s_n
            beside = (e * u_e + west * u_w) + (s * us[n, l, c, dn, :] + s_n * us[n, l, c, up, :])
            rest = k * u + (x if n else -x)
            inverse = 1.0 / diagonal
            ds[n, l, c, mid, :] = (rest + beside) * inverse - u
            ts[n, l, c, here, :] = inverse * BETA
            ws[n, l, c, here, :] = west
            before, now = now, after

    def sweep_2(n, l, at):
        here, mid, up, dn = (pl.ds(at + i, 8) for i in (0, PAD, PAD - 1, PAD + 1))

        def fetch(c):
            d = ds[n, l, c, mid, :]
            return d, pltpu.roll(d, LANES - 1, 1), pltpu.roll(d, 1, 1)

        before, now = (0.0,) * 3, fetch(0)
        for c in range(tiles):
            after = fetch(c + 1) if c + 1 < tiles else (0.0,) * 3
            d, d_e, d_w = now
            d_e = jnp.where(lane == LANES - 1, after[1], d_e)
            d_w = jnp.where(lane == 0, before[2], d_w)
            beside = (es[n, l, c, here, :] * d_e + ws[n, l, c, here, :] * d_w) + (
                ss[n, l, c, mid, :] * ds[n, l, c, dn, :] + ss[n, l, c, up, :] * ds[n, l, c, up, :]
            )
            out[n, l, c, here, :] = (us[n, l, c, mid, :] + ALPHA * d) + ts[n, l, c, here, :] * beside
            before, now = now, after

    def over(sweep, n, first, each, groups):
        def body(i, _):
            l = lax.div(i, groups)
            base = first + lax.rem(i, groups) * each
            for k in range(each):
                sweep(n, l, pl.multiple_of((base + k) * 8, 8))
            return 0

        lax.fori_loop(0, layers * groups, body, 0)

    def ends(n):
        def body(l, _):
            for o in (0, octets - 1):
                sweep_1(n, l, o * 8)
            return 0

        lax.fori_loop(0, layers, body, 0)

    for n in range(nets):
        ends(n)

    def turn(v, source, target):
        shift = (target - source) % LANES
        return pltpu.roll(v, shift, 1) if shift else v

    def in_columns(fix):
        def body(step, _):
            for k in range(FIX_STEP):
                at = pl.multiple_of(step * (8 * FIX_STEP) + k * 8, 8)
                for p, (n, l) in enumerate(planes):
                    fix(p, n, l, at)
            return 0

        lax.fori_loop(0, octets // FIX_STEP, body, 0)

    on(has_w, east_1.wait_recv)
    on(has_e, west_1.wait_recv)
    make_wide(0, col_w)
    make_wide(1, col_e)

    def join_columns(at, send):
        here, mid = pl.ds(at, 8), pl.ds(at + PAD, 8)
        c = tiles - 1
        to_e = jnp.zeros((8, LANES), f32)
        to_w = jnp.zeros((8, LANES), f32)
        from_e, from_w = col_e[here, :], col_w[here, :]
        fresh = []
        for p, (n, l) in enumerate(planes):
            gain = ts[n, l, c, here, :] * es[n, l, c, here, :] * (1.0 / BETA)
            final = ds[n, l, c, mid, :] + jnp.where(
                lane == LANES - 1, gain * turn(from_e, p, LANES - 1), 0.0
            )
            t, first, u = ts[n, l, 0, here, :], ds[n, l, 0, mid, :], us[n, l, 0, mid, :]
            edge = turn(from_w, len(planes) + p, 0)
            part = jnp.where(lane == 0, t * edge * (1.0 / BETA), 0.0)
            scale = 1.0 / (1.0 + part)
            first = (first + part * (turn(from_w, p, 0) - u)) * scale
            if send:
                to_e = jnp.where(lane == p, turn(final, LANES - 1, p), to_e)
                to_w = jnp.where(lane == p, turn(first, 0, p), to_w)
            fresh.append((n, l, final, first, t * scale))
        if send:
            snd_e2[here, :] = to_e
            snd_w2[here, :] = to_w
        for n, l, final, first, t in fresh:
            ds[n, l, c, mid, :] = final
            ds[n, l, 0, mid, :] = first
            ts[n, l, 0, here, :] = t

    for o in (0, octets - 1):
        join_columns(o * 8, False)
    on(has_s, south_d.start, south_t.start)
    on(has_n, north_d.start, north_t.start)

    for n in range(nets):
        over(sweep_1, n, 1, EACH_1, (octets - 2) // EACH_1)

    def join_inside(step, _):
        for k in range(FIX_INSIDE):
            join_columns(pl.multiple_of((1 + step * FIX_INSIDE + k) * 8, 8), True)
        return 0

    lax.fori_loop(0, (octets - 2) // FIX_INSIDE, join_inside, 0)

    die_1.wait_recv()
    link = [down[n][1] for n in range(nets)]
    outer = [[down[n][0], jnp.where(first_die, die_rcv[nets + n], 0.0)] for n in range(nets)]
    fresh = []
    for n, l in planes:
        beyond = die_rcv[n]
        if l == 0:
            beyond = jnp.where(first_die, 1.0 if n == 0 else 0.0, beyond)
        total = link[n] + outer[n][l]
        pull = link[n] * (held[n][1 - l] - held[n][l]) + outer[n][l] * (beyond - held[n][l])
        for c in range(tiles):
            t = ts[n, l, c, centres(0), :]
            a = t * (1.0 / BETA)
            scale = 1.0 / (1.0 + a * spread(total, c))
            fresh.append(
                (n, l, c, (ds[n, l, c, centres(PAD), :] + a * spread(pull, c)) * scale, t * scale)
            )
    for n, l, c, d, t in fresh:
        ds[n, l, c, centres(PAD), :] = d
        ts[n, l, c, centres(0), :] = t
    moved = [[gather_centres(ds, n, l) for l in range(layers)] for n in range(nets)]
    for n in range(nets):
        die_snd2[n] = jnp.where(first_die, moved[n][1], moved[n][0])

    die_2.start()

    on(has_n, south_u.wait_recv, south_s.wait_recv)
    on(has_s, north_u.wait_recv)
    on(has_s, south_d.wait_send, south_t.wait_send)
    on(has_n, north_d.wait_send, north_t.wait_send)
    fresh = []
    for n, l in planes:
        t, u = ts[n, l, :, 0, :], us[n, l, :, PAD, :]
        part = t * halo[n, l, :, N_S, :] * (1.0 / BETA)
        scale = 1.0 / (1.0 + part)
        gain = ts[n, l, :, rows - 1, :] * ss[n, l, :, last, :] * (1.0 / BETA)
        fresh.append(
            (
                n,
                l,
                (ds[n, l, :, PAD, :] + part * (halo[n, l, :, N_U, :] - u)) * scale,
                t * scale,
                ds[n, l, :, last, :] + gain * halo[n, l, :, S_U, :],
            )
        )
    for n, l, d, t, d_last in fresh:
        ds[n, l, :, PAD, :] = d
        ts[n, l, :, 0, :] = t
        ds[n, l, :, last, :] = d_last

    for o in (0, octets - 1):
        here, mid = slice(o * 8, o * 8 + 8), slice(o * 8 + PAD, o * 8 + PAD + 8)
        to_e = jnp.zeros((8, LANES), f32)
        to_w = jnp.zeros((8, LANES), f32)
        for p, (n, l) in enumerate(planes):
            to_e = jnp.where(lane == p, turn(ds[n, l, tiles - 1, mid, :], LANES - 1, p), to_e)
            to_w = jnp.where(lane == p, turn(ds[n, l, 0, mid, :], 0, p), to_w)
        snd_e2[here, :] = to_e
        snd_w2[here, :] = to_w
    make_thin(2, snd_e2)
    make_thin(3, snd_w2)
    on(has_e, east_2.start)
    on(has_w, west_2.start)

    for n in range(nets):
        over(sweep_2, n, 0, EACH_2, octets // EACH_2)

    die_2.wait_recv()
    fresh = []
    for n, l in planes:
        reach = outer[n][l] if l else jnp.where(first_die, 0.0, outer[n][l])
        pull = link[n] * moved[n][1 - l] + reach * die_rcv2[n]
        for c in range(tiles):
            value = out[n, l, c, centres(0), :] + ts[n, l, c, centres(0), :] * spread(pull, c)
            fresh.append((n, l, c, value))
    for n, l, c, value in fresh:
        out[n, l, c, centres(0), :] = value

    on(has_w, east_2.wait_recv)
    on(has_e, west_2.wait_recv)
    make_wide(2, col_w2)
    make_wide(3, col_e2)

    def join_columns_2(p, n, l, at):
        here = pl.ds(at, 8)
        c = tiles - 1
        gain = ts[n, l, c, here, :] * es[n, l, c, here, :]
        final = out[n, l, c, here, :] + jnp.where(
            lane == LANES - 1, gain * turn(col_e2[here, :], p, LANES - 1), 0.0
        )
        edge = turn(col_w[here, :], len(planes) + p, 0)
        first = out[n, l, 0, here, :] + jnp.where(
            lane == 0, ts[n, l, 0, here, :] * edge * turn(col_w2[here, :], p, 0), 0.0
        )
        out[n, l, c, here, :] = final
        out[n, l, 0, here, :] = first

    in_columns(join_columns_2)

    on(has_n, south_d.wait_recv, south_t.wait_recv)
    on(has_s, north_d.wait_recv, north_t.wait_recv)
    fresh = []
    for n, l in planes:
        north, south = halo[n, l, :, N_S, :], ss[n, l, :, last, :]
        d_n = halo[n, l, :, N_D, :] + halo[n, l, :, N_T, :] * (1.0 / BETA) * north * us[n, l, :, PAD, :]
        part = halo[n, l, :, S_T, :] * (1.0 / BETA) * south
        d_s = (halo[n, l, :, S_D, :] + part * (us[n, l, :, last, :] - halo[n, l, :, S_U, :])) / (
            1.0 + part
        )
        first = ts[n, l, :, 0, :] * north * d_n
        final = ts[n, l, :, rows - 1, :] * south * d_s
        fresh.append((n, l, out[n, l, :, 0, :] + first, out[n, l, :, rows - 1, :] + final))
    for n, l, first, final in fresh:
        out[n, l, :, 0, :] = first
        out[n, l, :, rows - 1, :] = final

    on(has_s, south_u.wait_send, south_s.wait_send)
    on(has_n, north_u.wait_send)
    on(has_e, east_1.wait_send, east_2.wait_send)
    on(has_w, west_1.wait_send, west_2.wait_send)
    die_1.wait_send()
    die_2.wait_send()


def store(cells, out, sem):
    nets, layers, tiles, _, _ = cells.shape
    copies = [
        pltpu.make_async_copy(
            cells.at[n, l, c], out.at[n, l, :, c * LANES : (c + 1) * LANES], sem.at[n, l, c]
        )
        for n in range(nets)
        for l in range(layers)
        for c in range(tiles)
    ]
    for copy in copies:
        copy.start()
    for copy in copies:
        copy.wait()


def local(u, k, e, s, sites, vias, patterns, pattern_currents):
    nets, layers, rows, cols = u.shape
    tiles = cols // LANES
    grid = (nets, layers, tiles, rows, LANES)
    padded = (nets, layers, tiles, rows + 2 * PAD, LANES)
    vmem = pltpu.VMEM
    hbm = pl.BlockSpec(memory_space=pltpu.HBM)
    on_chip = pl.BlockSpec(memory_space=vmem)
    column = vmem((rows, LANES), f32)
    packed = vmem((nets, 8, LANES), f32)
    limit = VMEM_LIMIT
    cells = pl.pallas_call(
        kernel,
        out_shape=vmem(grid, f32),
        in_specs=[hbm] * 8,
        out_specs=on_chip,
        scratch_shapes=[
            vmem(padded, f32), vmem(grid, f32), vmem(padded, f32), vmem(grid, f32),
            vmem(grid[1:], f32), vmem(padded, f32), vmem(grid, f32), vmem(grid, f32),
            vmem((nets, layers, tiles, 8, LANES), f32),
            pltpu.SMEM(sites.shape, jnp.int32), pltpu.SMEM(vias.shape, f32),
            vmem(patterns.shape, jnp.int32), vmem(pattern_currents.shape, f32), vmem((2,) + pattern_currents.shape[:1] + (8, LANES), f32),
            column, column, column, column, column, column, column, column,
            vmem((4, 16, LANES), f32), vmem((4, 16, LANES), f32),
            vmem((2 * nets, 8, LANES), f32), vmem((2 * nets, 8, LANES), f32), packed, packed,
            pltpu.SemaphoreType.DMA((5,)), pltpu.SemaphoreType.DMA((4,)),
            pltpu.SemaphoreType.DMA((13,)), pltpu.SemaphoreType.DMA((13,)),
        ],
        compiler_params=pltpu.CompilerParams(
            collective_id=0, has_side_effects=True, vmem_limit_bytes=limit
        ),
    )(u, k, e, s, sites, vias, patterns, pattern_currents)
    return pl.pallas_call(
        store,
        out_shape=jax.ShapeDtypeStruct(u.shape, f32),
        in_specs=[on_chip],
        out_specs=hbm,
        scratch_shapes=[pltpu.SemaphoreType.DMA((nets, layers, tiles))],
        compiler_params=pltpu.CompilerParams(vmem_limit_bytes=1024 * 1024),
    )(cells)


def solution(mesh):
    spec = P(None, "die", "row", "col")
    in_specs = (
        spec,
        spec,
        spec,
        spec,
        P("die", "row", "col", None),
        P(None, "die", "row", "col", None),
        P("die", "row", "col"),
        P(),
    )
    return jax.shard_map(local, mesh=mesh, in_specs=in_specs, out_specs=spec, check_vma=False)
```
